32 devices in a mesh: orb: 16 (over z, x, core), aux: 2 (over y).
Axes of the slice: x: 2, y: 2, z: 4, core: 2. Of those that a mesh axis runs over, the one named last changes fastest.
Arguments:
- three_index: float32 [56, 1024, 2048], P(None, 'aux', 'orb'), may hold values from -0.5 to 0.5
- pair_density: float32 [3136, 3136], P('orb'), as said below
- active_orbitals: int32 [56], replicated, may hold values from 200 to 2047, as said below
- screen_mask: int32 [64, 128], P('aux', 'orb'), may hold values from 0 to 1
- one_density: float32 [56, 56], replicated
- inactive_fock: float32 [2048, 256], P('orb'), may hold values from -6 to 6
- active_fock: float32 [2048, 200], P('orb'), may hold values from -6 to 6
Outputs:
- rotation_gradient: float32 [2048, 256], P(('orb', 'aux'))
The draws below stay inside these ranges and needn't reach their ends.
Inputs may be any that keep to these rules, and one draw needn't show every extreme that they name: `active_orbitals`: 56 distinct orbital indices. pair_density is symmetric: its entry at (tu, vw) equals that at (vw, tu).
All inputs are finite; a program needn't handle non-finite values.
Results may differ from the reference program's by a relative error of at most 0.0001.
Values sent between devices are 32-bit elements; how exact they have to be, the bound alone decides.
No kernel may reach another device: no remote copies, remote signals or barrier semaphores. Data moves between devices by JAX's collectives and lax.ppermute only.
A program may use at most 128 MiB of HBM per device.

```python
import jax
import jax.numpy as jnp
from jax import lax

ROWS_DEV = 128
NBF = 2048
NACT = 56
NPAIR = 3136
NINACT = 200
NOCC = 256
NAUX = 1024
AUXBLK = 16
SHELL = 16


def draw_pair_density(key, part):
    first, second = jax.random.split(jax.random.fold_in(key, 11))
    base = jax.random.normal(first, (NPAIR, NPAIR), jnp.float32)
    diag_values = jax.random.uniform(second, (NPAIR,), jnp.float32, 0.5, 1.5)
    rows_iota = jnp.arange(NPAIR)[:, None]
    cols_iota = jnp.arange(NPAIR)[None, :]
    diagonal = jnp.where(rows_iota == cols_iota, diag_values[:, None], 0.0)
    return (base + base.T) * (0.5 / NACT) + diagonal


def draw_one_density(key, part):
    first, second = jax.random.split(jax.random.fold_in(key, 23))
    base = 0.1 * jax.random.normal(first, (NACT, NACT), jnp.float32)
    diag_values = jax.random.uniform(second, (NACT,), jnp.float32, 0.2, 1.8)
    rows_iota = jnp.arange(NACT)[:, None]
    cols_iota = jnp.arange(NACT)[None, :]
    return base + base.T + jnp.where(rows_iota == cols_iota, diag_values[:, None], 0.0)


def draw_active_orbitals(key, part):
    order = jax.random.permutation(jax.random.fold_in(key, 37), NBF - NINACT)
    return (order[:NACT] + NINACT).astype(jnp.int32)


def draw_screen_mask(key, part):
    first, second = jax.random.split(jax.random.fold_in(key, 41))
    level = jax.random.randint(first, (1, NBF // ROWS_DEV), 1, 9)
    level = jnp.repeat(level, ROWS_DEV // SHELL, axis=1)
    draws = jax.random.randint(second, (NAUX // AUXBLK, NBF // SHELL), 0, 8)
    return (draws < level).astype(jnp.int32)


def block_levels(own_key, extent, shards, least, largest):
    loudness, own = 1.0, jax.random.fold_in(own_key, 6)
    for axis_at, blocks in shards:
        heights = jnp.exp(jax.random.uniform(jax.random.fold_in(own, axis_at), (blocks,), jnp.float32, least / len(shards), largest / len(shards)))
        loudness = loudness * jnp.repeat(heights, extent[axis_at] // blocks).reshape([-1 if axis == axis_at else 1 for axis in range(len(extent))])
    return loudness


def noise(own_key, dims, scale, reach, pieces=(), held_as=jnp.bfloat16):
    level = block_levels(own_key, dims, pieces, -0.22, 0.18) if pieces else 1.0
    entries = jax.random.normal(own_key, dims, jnp.float32) * scale * level
    return jnp.minimum(jnp.maximum(entries, -reach), reach).astype(held_as)


def setup_inputs(seed: int = 0) -> dict:
    splits = jax.random.split(jax.random.key(seed), 8)
    return {
        "three_index": noise(splits[0], (NACT, NAUX, NBF), 0.0625, 0.5, ((1, 2), (2, 16)), jnp.float32),
        "pair_density": draw_pair_density(jax.random.fold_in(splits[7], 71), 0),
        "active_orbitals": draw_active_orbitals(jax.random.fold_in(splits[7], 71), 0),
        "screen_mask": draw_screen_mask(jax.random.fold_in(splits[7], 71), 0),
        "one_density": draw_one_density(jax.random.fold_in(splits[7], 71), 0),
        "inactive_fock": noise(splits[5], (NBF, NOCC), 1.0, 6.0, ((0, 16),), jnp.float32),
        "active_fock": noise(splits[6], (NBF, NINACT), 1.0, 6.0, ((0, 16),), jnp.float32),
    }


def reference(three_index, pair_density, active_orbitals, screen_mask, one_density, inactive_fock, active_fock):
    highest = lax.Precision.HIGHEST
    kept_mask = jnp.repeat(jnp.repeat(screen_mask.astype(jnp.float32), AUXBLK, axis=0), SHELL, axis=1)
    active_rows = jnp.take(three_index, active_orbitals, axis=2)
    active_kept = jnp.take(kept_mask, active_orbitals, axis=1)
    pairs = (active_rows * active_kept[None, :, :]).transpose(1, 2, 0).reshape(NAUX, NPAIR)
    half = jnp.dot(pairs, pair_density, precision=highest)

    def aux_step(block_index, running):
        start = (block_index * AUXBLK).astype(jnp.int32)
        aux_piece = lax.dynamic_slice_in_dim(three_index, start, AUXBLK, 1)
        mask_piece = lax.dynamic_slice_in_dim(kept_mask, start, AUXBLK, 0)
        half_piece = lax.dynamic_slice_in_dim(half, start, AUXBLK, 0).reshape(AUXBLK, NACT, NACT)
        return running + jnp.einsum("uPp,Ptu->pt", aux_piece * mask_piece[None], half_piece, precision=highest)

    qmatrix = lax.fori_loop(0, NAUX // AUXBLK, aux_step, jnp.zeros((NBF, NACT), jnp.float32))
    inactive_cols = 2.0 * (inactive_fock[:, :NINACT] + active_fock)
    active_cols = jnp.dot(inactive_fock[:, NINACT:], one_density, precision=highest) + qmatrix
    fock = jnp.concatenate([inactive_cols, active_cols], axis=1)
    occ_index = jnp.concatenate([jnp.arange(NINACT).astype(jnp.int32), active_orbitals.astype(jnp.int32)])
    occupied = fock[occ_index]
    transposed = jnp.zeros((NBF, NOCC), jnp.float32).at[occ_index].set(occupied.T)
    return 2.0 * (fock - transposed)
```

```python
import functools

import jax
import jax.numpy as jnp
from jax import lax
from jax.experimental import pallas as pl
from jax.experimental.pallas import tpu as pltpu
from jax.sharding import PartitionSpec as P

HIGHEST = lax.Precision.HIGHEST
HIGH = lax.Precision.HIGH
LANES = 128
TILE = 8


def split(x):
    top = x.astype(jnp.bfloat16)
    return top, (x - top.astype(jnp.float32)).astype(jnp.bfloat16)


def mxu(a, b, contract):
    return lax.dot_general(a, b, (contract, ((), ())), preferred_element_type=jnp.float32)


def expand_mask(screen, quarter, chunk, rows):
    blocks, shells = screen.shape
    slab_rows = 4 * chunk // blocks
    row = lax.broadcasted_iota(jnp.int32, (chunk, blocks), 0) // slab_rows
    col = lax.broadcasted_iota(jnp.int32, (chunk, blocks), 1)
    down = (col == row + quarter * (blocks // 4)).astype(jnp.bfloat16)
    shell = lax.broadcasted_iota(jnp.int32, (shells, rows), 0)
    across = (shell == lax.broadcasted_iota(jnp.int32, (shells, rows), 1) // (rows // shells)).astype(jnp.bfloat16)
    nn = ((1,), (0,))
    tall = mxu(down, screen[...].astype(jnp.float32).astype(jnp.bfloat16), nn)
    return mxu(tall.astype(jnp.bfloat16), across, nn)


def extract_body(nb, info, active, three, screen, pairs, *refs):
    kept, pick, mask = refs[:-2], refs[-2], refs[-1]
    act, _, chunk = pairs.shape
    rows = three.shape[2]

    @pl.when(pl.program_id(0) == 0)
    def _():
        lane = lax.broadcasted_iota(jnp.int32, (1, rows), 1)
        for v in range(act):
            wanted = active[info[2 + v // nb] * nb + v % nb] - info[1]
            pick[v : v + 1, :rows] = (lane == wanted).astype(jnp.float32)
            pick[v : v + 1, rows:] = (lane == wanted).astype(jnp.float32)
        mask[...] = expand_mask(screen, info[0], chunk, rows)

    value = three[...] * mask[...][None]
    if kept:
        kept[0][...] = value
    top, low = split(value.reshape(TILE * chunk, rows))
    both = jnp.concatenate([top, low], axis=1)
    found = mxu(pick[...].astype(jnp.bfloat16), both, ((1,), (1,)))
    for w in range(TILE):
        pairs[:, w, :] = found[:, w * chunk : (w + 1) * chunk]


def extract(three_index, screen_mask, active, info, chunk, nb, keep):
    act, slab, rows = three_index.shape
    out_shape = [jax.ShapeDtypeStruct((act, act, chunk), jnp.float32)]
    out_specs = [pl.BlockSpec((act, TILE, chunk), lambda i, q, a: (0, i, 0))]
    if keep:
        out_shape.append(jax.ShapeDtypeStruct((act, chunk, rows), jnp.float32))
        out_specs.append(pl.BlockSpec((TILE, chunk, rows), lambda i, q, a: (i, 0, 0)))
    return pl.pallas_call(
        functools.partial(extract_body, nb),
        out_shape=out_shape,
        grid_spec=pltpu.PrefetchScalarGridSpec(
            num_scalar_prefetch=2,
            grid=(act // TILE,),
            in_specs=[
                pl.BlockSpec((TILE, chunk, rows), lambda i, q, a: (i, q[0], 0)),
                pl.BlockSpec(screen_mask.shape, lambda i, q, a: (0, 0)),
            ],
            out_specs=out_specs,
            scratch_shapes=[pltpu.VMEM((act, 2 * rows), jnp.float32), pltpu.VMEM((chunk, rows), jnp.float32)],
        ),
        cost_estimate=pl.CostEstimate(
            flops=4 * act * act * chunk * rows,
            transcendentals=0,
            bytes_accessed=4 * act * chunk * (act + rows * (2 if keep else 1)),
        ),
        name="extract",
    )(info, active, three_index, screen_mask)


def q_body(nb, info, three, screen, sib, *refs):
    blocks, out, lhs, acc, mask = refs[:-4], refs[-4], refs[-3], refs[-2], refs[-1]
    step = pl.program_id(0)
    rows = acc.shape[0]
    chunk = mask.shape[0]

    @pl.when(step == 0)
    def _():
        lhs[...] = jnp.zeros_like(lhs)
        acc[...] = jnp.zeros_like(acc)
        mask[...] = expand_mask(screen, info[0], chunk, mask.shape[1])

    for j, block in enumerate(blocks):
        for t in range(nb):
            lhs[pl.ds(j * TILE + t, TILE, stride=rows), :] = block[t]
    total = acc[...]
    for m in range(TILE // 2):
        pieces = [lhs[u * rows : (u + 1) * rows, :] for u in (2 * m, 2 * m + 1)]
        left, left_low = split(jnp.concatenate(pieces, axis=1))
        right = [jnp.concatenate([three[u] * mask[...], sib[u]], axis=1) for u in (2 * m, 2 * m + 1)]
        top, low = split(jnp.concatenate(right, axis=0))
        nn = ((1,), (0,))
        both = mxu(jnp.concatenate([left, left_low], axis=0), top, nn)
        total = total + (both[:rows] + both[rows:] + mxu(left, low, nn))
    acc[...] = total

    @pl.when(step == pl.num_programs(0) - 1)
    def _():
        for j in range(len(blocks)):
            where = pl.multiple_of(info[2 + j] * TILE, TILE)
            out[pl.ds(where, TILE), :] = acc[j * TILE : (j + 1) * TILE, :]


def q_partial(three_index, screen_mask, sib, blocks, info, chunk):
    act, slab, rows = three_index.shape
    count = len(blocks)
    nb = act // count
    in_specs = [
        pl.BlockSpec((TILE, chunk, rows), lambda i, q: (i, q[0], 0)),
        pl.BlockSpec(screen_mask.shape, lambda i, q: (0, 0)),
        pl.BlockSpec((TILE, chunk, rows), lambda i, q: (i, 0, 0)),
    ] + [pl.BlockSpec((nb, TILE, chunk), lambda i, q: (0, i, 0))] * count
    return pl.pallas_call(
        functools.partial(q_body, nb),
        out_shape=jax.ShapeDtypeStruct((count * TILE, 2 * rows), jnp.float32),
        grid_spec=pltpu.PrefetchScalarGridSpec(
            num_scalar_prefetch=1,
            grid=(act // TILE,),
            in_specs=in_specs,
            out_specs=pl.BlockSpec((count * TILE, 2 * rows), lambda i, q: (0, 0)),
            scratch_shapes=[
                pltpu.VMEM((TILE * count * TILE, chunk), jnp.float32),
                pltpu.VMEM((count * TILE, 2 * rows), jnp.float32),
                pltpu.VMEM((chunk, rows), jnp.float32),
            ],
        ),
        cost_estimate=pl.CostEstimate(
            flops=12 * act * act * chunk * rows,
            transcendentals=0,
            bytes_accessed=4 * act * chunk * (act + 2 * rows),
        ),
        name="qpartial",
    )(info, three_index, screen_mask, sib, *[b.reshape(nb, act, chunk) for b in blocks])


def fast(orb, aux, three_index, pair_density, active_orbitals, screen_mask, one_density, inactive_fock, active_fock):
    act, slab, rows = three_index.shape
    inactive = active_fock.shape[1]
    chips = orb // 2
    nb = act // chips
    blk = nb * act
    chunk = slab // 4
    me = lax.axis_index("orb")
    chip, core = me // 2, me % 2
    sign = 1 - 2 * core
    first_row = me * rows

    order = list(range(0, chips, 2)) + list(range(chips - 1, 0, -2))
    position = jnp.where(chip % 2 == 0, chip // 2, (2 * chips - 1 - chip) // 2)

    def info_of(sgn, half, k):
        place = (position + sgn * jnp.arange(chips, dtype=jnp.int32) + chips) % chips
        by_hops = jnp.where(place < chips // 2, 2 * place, 2 * chips - 1 - 2 * place)
        return jnp.concatenate([(2 * half + k).reshape(1), first_row.reshape(1), by_hops]).astype(jnp.int32)

    near = [(order[k], order[(k + 1) % chips]) for k in range(chips)]
    ahead = [(2 * a, 2 * b) for a, b in near] + [(2 * b + 1, 2 * a + 1) for a, b in near]
    behind = [(b, a) for a, b in ahead]
    twin = [(i, i ^ 1) for i in range(orb)]

    def hop(x, pairs):
        return lax.ppermute(x, "orb", pairs)

    local_rows = jnp.arange(rows, dtype=jnp.int32)
    mine = [info_of(sign, core, k) for k in range(2)]
    theirs = [info_of(-sign, 1 - core, k) for k in range(2)]

    contributions, sib_three = [], []
    for k in range(2):
        given, kept = extract(three_index, screen_mask, active_orbitals, theirs[k], chunk, nb, True)
        (own,) = extract(three_index, screen_mask, active_orbitals, mine[k], chunk, nb, False)
        got = hop(given.reshape(act * act, chunk), twin)
        own = own.reshape(act * act, chunk)
        contributions.append([own[j * blk : (j + 1) * blk] + got[j * blk : (j + 1) * blk] for j in range(chips)])
        sib_three.append(hop(kept, twin))
        if k == 0:
            inactive_fock, active_fock, pair_density, own = lax.optimization_barrier(
                (inactive_fock, active_fock, pair_density, own)
            )

    other = hop(pair_density, twin)
    density = jnp.concatenate(
        [jnp.where(core == 0, pair_density, other), jnp.where(core == 0, other, pair_density)], axis=0
    )
    density_rel = [lax.dynamic_slice_in_dim(density, mine[0][2 + j] * blk, blk, 1) for j in range(chips)]

    occ_index = jnp.concatenate([jnp.arange(inactive, dtype=jnp.int32), active_orbitals])
    occ_pick = ((first_row + local_rows)[:, None] == occ_index[None, :]).astype(jnp.float32)
    fixed = jnp.concatenate(
        [
            2.0 * (inactive_fock[:, :inactive] + active_fock),
            jnp.dot(inactive_fock[:, inactive:], one_density, precision=HIGHEST),
        ],
        axis=1,
    )
    occupied_fixed = lax.psum(jnp.dot(occ_pick.T, fixed, precision=HIGHEST), "orb")

    far = chips // 2
    totals = []
    for k in range(2):
        c = contributions[k]
        a = hop(c[far], ahead)
        b = hop(c[far + 1], behind) if chips - 1 - far > 0 else None
        for s in range(1, far):
            a = hop(a + c[far - s], ahead)
            if s < chips - 1 - far:
                b = hop(b + c[far + 1 + s], behind)
        totals.append(c[0] + a + b)

    def gather(x):
        blocks = [None] * chips
        blocks[0] = a = b = x
        for s in range(1, far + 1):
            a = hop(a, ahead)
            blocks[(chips - s) % chips] = a
            if s < chips - far:
                b = hop(b, behind)
                blocks[s] = b
        return blocks

    q = 0.0
    for k in range(2):
        pair_blocks = gather(totals[k])
        half = 0.0
        for j in [0] + [n for s in range(1, far + 1) for n in ((chips - s), s)][: chips - 1]:
            half = half + jnp.dot(density_rel[j], pair_blocks[j], precision=HIGH)
        if k == 0:
            half, occupied_fixed = lax.optimization_barrier((half, occupied_fixed))
        half_blocks = gather(half)
        q = q + q_partial(three_index, screen_mask, sib_three[k], half_blocks, mine[k], chunk)
    q = q.reshape(chips, TILE, 2 * rows)[:, :nb].reshape(act, 2 * rows)

    share = rows // aux
    aux_at = lax.axis_index("aux")

    def both(x, orb_bits, aux_bits):
        table = [(o * aux + y, (o ^ orb_bits) * aux + (y ^ aux_bits)) for o in range(orb) for y in range(aux)]
        return x + lax.ppermute(x, ("orb", "aux"), table)

    swapped = jnp.concatenate([q[:, rows:], q[:, :rows]], axis=1)
    q = q + lax.ppermute(swapped, "orb", twin)
    q = both(q, 0, 1)
    q_mine = q[:, :rows]
    q_rows = lax.dynamic_slice_in_dim(q_mine, aux_at * share, share, 1)

    other_row = (me ^ 1) * rows
    chip_rows = jnp.concatenate([first_row + local_rows, other_row + local_rows])
    chip_pick = (chip_rows[:, None] == occ_index[None, :]).astype(jnp.float32)
    occ_q = jnp.dot(q, chip_pick, precision=HIGHEST)
    for bit in (2, 4, 8):
        occ_q = both(occ_q, bit, 0)
    occupied = occupied_fixed + jnp.pad(occ_q.T, ((0, 0), (inactive, 0)))

    fixed_mine = lax.dynamic_slice_in_dim(fixed, aux_at * share, share, 0)
    pick_rows = lax.dynamic_slice_in_dim(occ_pick, aux_at * share, share, 0)
    fock_mine = fixed_mine + jnp.pad(q_rows.T, ((0, 0), (inactive, 0)))
    transposed = jnp.dot(pick_rows, occupied.T, precision=HIGHEST)
    return 2.0 * (fock_mine - transposed)


def plain(orb, aux, three_index, pair_density, active_orbitals, screen_mask, one_density, inactive_fock, active_fock):
    act_count = three_index.shape[0]
    slab_count = three_index.shape[1]
    row_count = three_index.shape[2]
    inactive_count = active_fock.shape[1]
    orb_position = lax.axis_index("orb")
    kept_mask = jnp.repeat(
        jnp.repeat(screen_mask.astype(jnp.float32), slab_count // screen_mask.shape[0], axis=0),
        row_count // screen_mask.shape[1],
        axis=1,
    )
    screened = three_index * kept_mask[None]
    global_rows = orb_position * row_count + jnp.arange(row_count, dtype=jnp.int32)
    active_pick = (global_rows[:, None] == active_orbitals[None, :]).astype(jnp.float32)
    partial_pairs = jnp.einsum("wPp,pv->Pvw", screened, active_pick, precision=HIGHEST).reshape(
        slab_count, act_count * act_count
    )
    pairs = lax.psum(partial_pairs, "orb")
    column_block = jnp.dot(pairs, pair_density.T, precision=HIGHEST)
    half = lax.all_gather(column_block, "orb", axis=1, tiled=True)
    q_partial = jnp.einsum(
        "uPp,Ptu->pt", screened, half.reshape(slab_count, act_count, act_count), precision=HIGHEST
    )
    occ_index = jnp.concatenate([jnp.arange(inactive_count, dtype=jnp.int32), active_orbitals])
    row_share = row_count // aux
    aux_offset = lax.axis_index("aux") * row_share
    qmatrix = lax.psum(q_partial, "aux")
    inactive_cols = 2.0 * (inactive_fock[:, :inactive_count] + active_fock)
    active_cols = jnp.dot(inactive_fock[:, inactive_count:], one_density, precision=HIGHEST) + qmatrix
    fock = jnp.concatenate([inactive_cols, active_cols], axis=1)
    occ_pick = (global_rows[:, None] == occ_index[None, :]).astype(jnp.float32)
    occupied = lax.psum(jnp.dot(occ_pick.T, fock, precision=HIGHEST), "orb")
    fock_mine = lax.dynamic_slice_in_dim(fock, aux_offset, row_share, 0)
    pick_mine = lax.dynamic_slice_in_dim(occ_pick, aux_offset, row_share, 0)
    transposed = jnp.dot(pick_mine, occupied.T, precision=HIGHEST)
    return 2.0 * (fock_mine - transposed)


def shards(orb, aux, *args):
    act, slab, rows = args[0].shape
    chips = orb // 2
    fits = orb == 16 and aux == 2 and act % chips == 0 and act % TILE == 0
    fits = fits and slab % (4 * LANES) == 0 and rows % LANES == 0
    return (fast if fits else plain)(orb, aux, *args)


def solution(mesh):
    in_specs = (
        P(None, "aux", "orb"),
        P("orb", None),
        P(),
        P("aux", "orb"),
        P(),
        P("orb", None),
        P("orb", None),
    )
    out_specs = P(("orb", "aux"), None)
    body = functools.partial(shards, mesh.shape["orb"], mesh.shape["aux"])
    return jax.shard_map(body, mesh=mesh, in_specs=in_specs, out_specs=out_specs, check_vma=False)
```

```python
import functools

import jax
import jax.numpy as jnp
from jax import lax
from jax.experimental import pallas as pl
from jax.experimental.pallas import tpu as pltpu
from jax.sharding import PartitionSpec as P

HIGHEST = lax.Precision.HIGHEST
HIGH = lax.Precision.HIGH
LANES = 128
TILE = 8
MIB = 1024 * 1024


def split(x):
    top = x.astype(jnp.bfloat16)
    return top, (x - top.astype(jnp.float32)).astype(jnp.bfloat16)


def mxu(a, b, contract):
    return lax.dot_general(a, b, (contract, ((), ())), preferred_element_type=jnp.float32)


def places():
    return tuple(pl.BlockSpec(memory_space=m) for m in (pltpu.SMEM, pltpu.VMEM, pltpu.HBM, pl.ANY))


def expand_mask(screen, quarter, chunk, rows):
    shells, blocks = screen.shape
    slab_rows = 4 * chunk // blocks
    row = lax.broadcasted_iota(jnp.int32, (chunk, blocks), 0) // slab_rows
    col = lax.broadcasted_iota(jnp.int32, (chunk, blocks), 1)
    down = (col == row + quarter * (blocks // 4)).astype(jnp.bfloat16)
    shell = lax.broadcasted_iota(jnp.int32, (shells, rows), 0)
    across = (shell == lax.broadcasted_iota(jnp.int32, (shells, rows), 1) // (rows // shells)).astype(jnp.bfloat16)
    tall = mxu(down, screen[...].astype(jnp.float32).astype(jnp.bfloat16), ((1,), (1,)))
    return mxu(tall.astype(jnp.bfloat16), across, ((1,), (0,)))


def extract_body(nb, info, active, three, screen, pairs, *refs):
    kept = refs[0] if len(refs) == 8 else None
    value, turned, found, mask, sem_in, sem_out, sem_kept = refs[-7:]
    act = pairs.shape[0]
    _, chunk, rows = value.shape
    tiles = act // TILE
    start = pl.multiple_of(info[0] * chunk, chunk)

    def tile(i):
        return pl.ds(pl.multiple_of(i * TILE, TILE), TILE)

    def fetch(i):
        return pltpu.make_async_copy(three.at[tile(i), pl.ds(start, chunk), :], value.at[tile(i)], sem_in.at[i])

    def keep(i):
        return pltpu.make_async_copy(value.at[tile(i)], kept.at[tile(i)], sem_kept.at[i])

    for i in range(tiles):
        fetch(i).start()
    mask[...] = expand_mask(screen, info[0], chunk, rows)

    found[...] = jnp.zeros_like(found)

    @pl.loop(0, tiles)
    def _(i):
        fetch(i).wait()
        part = value[tile(i)] * mask[...][None]
        if kept is not None:
            value[tile(i)] = part
            keep(i).start()
        for w in range(TILE):
            turned[pl.ds(pl.multiple_of((i * TILE + w) * rows, rows), rows), :] = part[w].T

    for v in range(act):
        row = active[info[2 + v // nb] * nb + v % nb] - info[1]

        @pl.when(jnp.logical_and(row >= 0, row < rows))
        def _():
            for i in range(tiles):
                lines = turned[pl.ds(i * TILE * rows + row, TILE, stride=rows), :]
                found[v, i * TILE : (i + 1) * TILE, :] = lines

    give = pltpu.make_async_copy(found, pairs, sem_out)
    give.start()
    give.wait()
    if kept is not None:
        for i in range(tiles):
            keep(i).wait()


def extract(three_index, screen_mask, active, info, chunk, nb, keep):
    act, slab, rows = three_index.shape
    tiles = act // TILE
    out_shape = [jax.ShapeDtypeStruct((act, act, chunk), jnp.float32)]
    if keep:
        out_shape.append(jax.ShapeDtypeStruct((act, chunk, rows), jnp.float32))
    smem, vmem, hbm, anywhere = places()
    return pl.pallas_call(
        functools.partial(extract_body, nb),
        out_shape=out_shape,
        in_specs=[smem, smem, hbm, vmem],
        out_specs=[anywhere] * len(out_shape),
        scratch_shapes=[
            pltpu.VMEM((act, chunk, rows), jnp.float32),
            pltpu.VMEM((act * rows, chunk), jnp.float32),
            pltpu.VMEM((act, act, chunk), jnp.float32),
            pltpu.VMEM((chunk, rows), jnp.float32),
            pltpu.SemaphoreType.DMA((tiles,)),
            pltpu.SemaphoreType.DMA,
            pltpu.SemaphoreType.DMA((tiles,)),
        ],
        compiler_params=pltpu.CompilerParams(vmem_limit_bytes=52 * MIB),
        cost_estimate=pl.CostEstimate(
            flops=4 * act * act * chunk * rows,
            transcendentals=0,
            bytes_accessed=4 * act * chunk * (act + rows * (2 if keep else 1)),
        ),
        name="extract",
    )(info, active, three_index, screen_mask)


def q_body(nb, count, info, three, screen, sib, *refs):
    blocks = refs[:count]
    out, own_s, sib_s, held, lhs, acc, mask, sem_own, sem_sib, sem_block = refs[count:]
    act, chunk, rows = own_s.shape
    tiles = act // TILE
    height = acc.shape[0]
    start = pl.multiple_of(info[0] * chunk, chunk)

    def tile(i):
        return pl.ds(pl.multiple_of(i * TILE, TILE), TILE)

    def own(i):
        return pltpu.make_async_copy(three.at[tile(i), pl.ds(start, chunk), :], own_s.at[tile(i)], sem_own.at[i])

    def other(i):
        return pltpu.make_async_copy(sib.at[tile(i)], sib_s.at[tile(i)], sem_sib.at[i])

    def bring(j):
        return pltpu.make_async_copy(blocks[j], held.at[j], sem_block.at[j])

    for j in range(count):
        bring(j).start()
    for i in range(tiles):
        own(i).start()
        other(i).start()
    lhs[...] = jnp.zeros_like(lhs)
    mask[...] = expand_mask(screen, info[0], chunk, rows)
    for j in range(count):
        bring(j).wait()
    acc[...] = jnp.zeros_like(acc)
    nn = ((1,), (0,))

    @pl.loop(0, tiles)
    def _(i):
        for j in range(count):
            for t in range(nb):
                lhs[pl.ds(j * TILE + t, TILE, stride=height), :] = held[j, t, tile(i), :]
        own(i).wait()
        other(i).wait()
        total = acc[...]
        for m in range(0, TILE, 2):
            pieces = [lhs[n * height : (n + 1) * height, :] for n in (m, m + 1)]
            left, left_low = split(jnp.concatenate(pieces, axis=1))
            right = [jnp.concatenate([own_s[i * TILE + n] * mask[...], sib_s[i * TILE + n]], axis=1) for n in (m, m + 1)]
            top, low = split(jnp.concatenate(right, axis=0))
            both = mxu(jnp.concatenate([left, left_low], axis=0), top, nn)
            total = total + (both[:height] + both[height:] + mxu(left, low, nn))
        acc[...] = total

    for j in range(count):
        where = pl.multiple_of(info[2 + j] * TILE, TILE)
        out[pl.ds(where, TILE), :] = acc[j * TILE : (j + 1) * TILE, :]


def q_partial(three_index, screen_mask, sib, blocks, info, chunk):
    act, slab, rows = three_index.shape
    count = len(blocks)
    nb = act // count
    tiles = act // TILE
    smem, vmem, hbm, anywhere = places()
    return pl.pallas_call(
        functools.partial(q_body, nb, count),
        out_shape=jax.ShapeDtypeStruct((count * TILE, 2 * rows), jnp.float32),
        in_specs=[smem, hbm, vmem, anywhere] + [anywhere] * count,
        out_specs=vmem,
        scratch_shapes=[
            pltpu.VMEM((act, chunk, rows), jnp.float32),
            pltpu.VMEM((act, chunk, rows), jnp.float32),
            pltpu.VMEM((count, nb, act, chunk), jnp.float32),
            pltpu.VMEM((TILE * count * TILE, chunk), jnp.float32),
            pltpu.VMEM((count * TILE, 2 * rows), jnp.float32),
            pltpu.VMEM((chunk, rows), jnp.float32),
            pltpu.SemaphoreType.DMA((tiles,)),
            pltpu.SemaphoreType.DMA((tiles,)),
            pltpu.SemaphoreType.DMA((count,)),
        ],
        compiler_params=pltpu.CompilerParams(vmem_limit_bytes=52 * MIB),
        cost_estimate=pl.CostEstimate(
            flops=12 * act * act * chunk * rows,
            transcendentals=0,
            bytes_accessed=4 * act * chunk * (act + 2 * rows),
        ),
        name="qpartial",
    )(info, three_index, screen_mask, sib, *[b.reshape(nb, act, chunk) for b in blocks])


def half_body(chips, info, own, twin, *refs):
    count = 2 * (chips - 1)
    blocks, outs = refs[:count], refs[count : count + 2]
    density, held, acc, sem_own, sem_twin, sem_block = refs[count + 2 :]
    size, chunk = blocks[0].shape
    rows, depth = own.shape
    core = info[2 + chips]

    def bring(n):
        j, k = n // 2, n % 2
        hops = j if j < chips // 2 else j + 1
        where = pl.ds(pl.multiple_of(info[2 + hops] * size, TILE), size)
        return pltpu.make_async_copy(blocks[n], held.at[where, pl.ds(k * chunk, chunk)], sem_block.at[n])

    mine = pltpu.make_async_copy(own, density.at[core], sem_own)
    other = pltpu.make_async_copy(twin, density.at[1 - core], sem_twin)
    mine.start()
    other.start()
    for n in range(count):
        bring(n).start()
    missing = pl.ds(pl.multiple_of(info[2 + chips // 2] * size, TILE), size)
    held[missing, :] = jnp.zeros((size, 2 * chunk), jnp.float32)
    acc[...] = jnp.zeros_like(acc)
    mine.wait()
    other.wait()
    for n in range(count):
        bring(n).wait()
    nn = ((1,), (0,))
    step = 2 * LANES

    def add(start, length):
        top, low = split(held[pl.ds(start, length), :])
        for h in range(2):
            left, left_low = split(density[h, :, pl.ds(start, length)])
            acc[h] += mxu(left, top, nn) + mxu(left_low, top, nn) + mxu(left, low, nn)

    @pl.loop(0, depth // step)
    def _(i):
        add(pl.multiple_of(i * step, step), step)

    if depth % step:
        add(depth - depth % step, depth % step)
    for k in range(2):
        for h in range(2):
            outs[k][h * rows : (h + 1) * rows, :] = acc[h, :, k * chunk : (k + 1) * chunk]


def half_partial(own, twin, blocks, info, chips):
    size, chunk = blocks[0].shape
    rows, depth = own.shape
    smem, vmem, hbm, anywhere = places()
    return pl.pallas_call(
        functools.partial(half_body, chips),
        out_shape=[jax.ShapeDtypeStruct((2 * rows, chunk), jnp.float32)] * 2,
        in_specs=[smem, anywhere, anywhere] + [anywhere] * len(blocks),
        out_specs=[vmem, vmem],
        scratch_shapes=[
            pltpu.VMEM((2, rows, depth), jnp.float32),
            pltpu.VMEM((depth, 2 * chunk), jnp.float32),
            pltpu.VMEM((2, rows, 2 * chunk), jnp.float32),
            pltpu.SemaphoreType.DMA,
            pltpu.SemaphoreType.DMA,
            pltpu.SemaphoreType.DMA((len(blocks),)),
        ],
        compiler_params=pltpu.CompilerParams(vmem_limit_bytes=16 * MIB),
        cost_estimate=pl.CostEstimate(
            flops=24 * rows * depth * chunk,
            transcendentals=0,
            bytes_accessed=8 * rows * depth + 8 * depth * chunk,
        ),
        name="half",
    )(info, own, twin, *blocks)


def fast(orb, aux, three_index, pair_density, active_orbitals, screen_mask, one_density, inactive_fock, active_fock):
    act, slab, rows = three_index.shape
    inactive = active_fock.shape[1]
    chips = orb // 2
    nb = act // chips
    blk = nb * act
    chunk = slab // 4
    me = lax.axis_index("orb")
    chip, core = lax.shift_right_logical(me, 1), lax.bitwise_and(me, 1)
    half_chip = lax.shift_right_logical(chip, 1)
    sign = 1 - 2 * core
    first_row = me * rows

    order = list(range(0, chips, 2)) + list(range(chips - 1, 0, -2))
    position = jnp.where(lax.bitwise_and(chip, 1) == 0, half_chip, chips - 1 - half_chip)

    def chip_at(sgn, hops):
        place = lax.rem(position + sgn * hops + chips, chips)
        return jnp.where(place < chips // 2, 2 * place, 2 * chips - 1 - 2 * place)

    def info_of(sgn, half, k):
        by_hops = chip_at(sgn, jnp.arange(chips, dtype=jnp.int32))
        return jnp.concatenate([jnp.stack([2 * half + k, first_row]), by_hops, core.reshape(1)]).astype(jnp.int32)

    near = [(order[k], order[(k + 1) % chips]) for k in range(chips)]
    ahead = [(2 * a, 2 * b) for a, b in near] + [(2 * b + 1, 2 * a + 1) for a, b in near]
    behind = [(b, a) for a, b in ahead]
    twin = [(i, i ^ 1) for i in range(orb)]

    def hop(x, pairs):
        return lax.ppermute(x, "orb", pairs)

    local_rows = jnp.arange(rows, dtype=jnp.int32)
    mine = [info_of(sign, core, k) for k in range(2)]
    theirs = [info_of(-sign, 1 - core, k) for k in range(2)]

    shells = screen_mask.T
    contributions, sib_three = [], []
    for k in range(2):
        given, kept = extract(three_index, shells, active_orbitals, theirs[k], chunk, nb, True)
        (own,) = extract(three_index, shells, active_orbitals, mine[k], chunk, nb, False)
        got = hop(given.reshape(act * act, chunk), twin)
        own = own.reshape(act * act, chunk)
        sums = [own[j * blk : (j + 1) * blk] + got[j * blk : (j + 1) * blk] for j in range(chips)]
        sib_three.append(kept)
        if k == 0:
            theirs[1], mine[1], sums[chips // 2] = lax.optimization_barrier((theirs[1], mine[1], sums[chips // 2]))
        else:
            pair_density, inactive_fock, active_fock, sib_three, sums[chips // 2] = lax.optimization_barrier(
                (pair_density, inactive_fock, active_fock, sib_three, sums[chips // 2])
            )
        contributions.append(sums)

    other = hop(pair_density, twin)
    sib_three = [hop(x, twin) for x in sib_three]
    far = chips // 2
    first = [(hop(c[far], ahead), hop(c[far + 1], behind)) for c in contributions]
    first, other, sib_three = lax.optimization_barrier((first, other, sib_three))
    totals = []
    for c, (a, b) in zip(contributions, first):
        for s in range(1, far):
            a = hop(a + c[far - s], ahead)
            if s < chips - 1 - far:
                b = hop(b + c[far + 1 + s], behind)
        totals.append(c[0] + a + b)
    totals = lax.optimization_barrier(totals)

    far_at = chip_at(sign, far) * blk
    far_columns = [lax.dynamic_slice_in_dim(d, far_at, blk, 1) for d in (pair_density, other)]
    density_far = jnp.concatenate(
        [jnp.where(core == 0, far_columns[0], far_columns[1]), jnp.where(core == 0, far_columns[1], far_columns[0])],
        axis=0,
    )

    def gather(x):
        blocks = [None] * chips
        blocks[0] = a = b = x
        for s in range(1, far + 1):
            a = hop(a, ahead)
            blocks[(chips - s) % chips] = a
            if s < chips - far:
                b = hop(b, behind)
                blocks[s] = b
        return blocks

    gathered = [gather(x) for x in totals]
    near_blocks = [gathered[k][j] for j in range(chips) if j != far for k in range(2)]
    halves = half_partial(pair_density, other, near_blocks, mine[0], chips)
    halves = [h + jnp.dot(density_far, gathered[k][far], precision=HIGH) for k, h in enumerate(halves)]
    halves = lax.optimization_barrier(halves)
    q = 0.0
    for k, x in enumerate(halves):
        q = q + q_partial(three_index, shells, sib_three[k], gather(x), mine[k], chunk)
    q = q.reshape(chips, TILE, 2 * rows)[:, :nb].reshape(act, 2 * rows)

    share = rows // aux
    aux_at = lax.axis_index("aux")

    def across(x, orb_bits, aux_bits):
        table = [(o * aux + y, (o ^ orb_bits) * aux + (y ^ aux_bits)) for o in range(orb) for y in range(aux)]
        return lax.ppermute(x, ("orb", "aux"), table)

    closed = 2.0 * (inactive_fock[:, :inactive] + active_fock)
    opened = jnp.dot(inactive_fock[:, inactive:], one_density, precision=HIGHEST)
    closed_twin = hop(closed, twin)
    closed_chip = jnp.concatenate(
        [jnp.where(core == 0, closed, closed_twin), jnp.where(core == 0, closed_twin, closed)], axis=0
    )

    once = (aux_at == 0).astype(jnp.float32)
    own_q, twin_q = q[:, :rows] + once * opened.T, q[:, rows:]
    q_mine = own_q + hop(twin_q, twin)
    sent = lax.dynamic_slice_in_dim(q_mine, (1 - aux_at) * share, share, 1)
    q_rows = lax.dynamic_slice_in_dim(q_mine, aux_at * share, share, 1) + across(sent, 0, 1)

    occ_index = jnp.concatenate([jnp.arange(inactive, dtype=jnp.int32), active_orbitals])
    my_rows, twin_rows = first_row + local_rows, (me ^ 1) * rows + local_rows
    width = (inactive + act) // 2
    act_pick = (active_orbitals[:, None] == my_rows[None, :]).astype(jnp.float32) * once
    act_closed = jnp.pad(jnp.dot(act_pick, closed, precision=HIGHEST), ((0, 0), (0, act)))

    def picked(half):
        wanted = lax.dynamic_slice_in_dim(occ_index, half * width, width, 0)
        chosen = [(r[:, None] == wanted[None, :]).astype(jnp.float32) for r in (my_rows, twin_rows)]
        top = jnp.dot(jnp.concatenate([own_q, twin_q], axis=1), jnp.concatenate(chosen, axis=0), precision=HIGHEST)
        return jnp.concatenate([top, lax.dynamic_slice_in_dim(act_closed, half * width, width, 1)], axis=0)

    occ = picked(core) + hop(picked(1 - core), twin)
    occ = occ + across(occ, 2, 0) + across(occ, 0, 1) + across(occ, 2, 1)
    occ = occ + across(occ, 4, 0) + across(occ, 8, 0) + across(occ, 12, 0)
    occ_twin = hop(occ, twin)
    occ = jnp.concatenate([jnp.where(core == 0, occ, occ_twin), jnp.where(core == 0, occ_twin, occ)], axis=1)

    upper = jnp.concatenate([closed_chip[:inactive].T, occ[act:, :inactive].T], axis=1)
    occupied = jnp.concatenate([upper, occ[:act]], axis=0)

    mine_at = aux_at * share
    fock_mine = jnp.concatenate([lax.dynamic_slice_in_dim(closed, mine_at, share, 0), q_rows.T], axis=1)
    pick_rows = (first_row + mine_at + jnp.arange(share, dtype=jnp.int32))[:, None] == occ_index[None, :]
    transposed = jnp.dot(pick_rows.astype(jnp.float32), occupied, precision=HIGHEST)
    return 2.0 * (fock_mine - transposed)


def plain(orb, aux, three_index, pair_density, active_orbitals, screen_mask, one_density, inactive_fock, active_fock):
    act_count = three_index.shape[0]
    slab_count = three_index.shape[1]
    row_count = three_index.shape[2]
    inactive_count = active_fock.shape[1]
    orb_position = lax.axis_index("orb")
    kept_mask = jnp.repeat(
        jnp.repeat(screen_mask.astype(jnp.float32), slab_count // screen_mask.shape[0], axis=0),
        row_count // screen_mask.shape[1],
        axis=1,
    )
    screened = three_index * kept_mask[None]
    global_rows = orb_position * row_count + jnp.arange(row_count, dtype=jnp.int32)
    active_pick = (global_rows[:, None] == active_orbitals[None, :]).astype(jnp.float32)
    partial_pairs = jnp.einsum("wPp,pv->Pvw", screened, active_pick, precision=HIGHEST).reshape(
        slab_count, act_count * act_count
    )
    pairs = lax.psum(partial_pairs, "orb")
    column_block = jnp.dot(pairs, pair_density.T, precision=HIGHEST)
    half = lax.all_gather(column_block, "orb", axis=1, tiled=True)
    q_partial = jnp.einsum(
        "uPp,Ptu->pt", screened, half.reshape(slab_count, act_count, act_count), precision=HIGHEST
    )
    occ_index = jnp.concatenate([jnp.arange(inactive_count, dtype=jnp.int32), active_orbitals])
    row_share = row_count // aux
    aux_offset = lax.axis_index("aux") * row_share
    qmatrix = lax.psum(q_partial, "aux")
    inactive_cols = 2.0 * (inactive_fock[:, :inactive_count] + active_fock)
    active_cols = jnp.dot(inactive_fock[:, inactive_count:], one_density, precision=HIGHEST) + qmatrix
    fock = jnp.concatenate([inactive_cols, active_cols], axis=1)
    occ_pick = (global_rows[:, None] == occ_index[None, :]).astype(jnp.float32)
    occupied = lax.psum(jnp.dot(occ_pick.T, fock, precision=HIGHEST), "orb")
    fock_mine = lax.dynamic_slice_in_dim(fock, aux_offset, row_share, 0)
    pick_mine = lax.dynamic_slice_in_dim(occ_pick, aux_offset, row_share, 0)
    transposed = jnp.dot(pick_mine, occupied.T, precision=HIGHEST)
    return 2.0 * (fock_mine - transposed)


def shards(orb, aux, *args):
    act, slab, rows = args[0].shape
    chips = orb // 2
    fits = orb == 16 and aux == 2 and act % chips == 0 and act % TILE == 0
    fits = fits and args[6].shape[1] <= 2 * rows and (args[6].shape[1] + act) % 2 == 0
    fits = fits and slab % (4 * LANES) == 0 and rows % LANES == 0
    return (fast if fits else plain)(orb, aux, *args)


def solution(mesh):
    in_specs = (
        P(None, "aux", "orb"),
        P("orb", None),
        P(),
        P("aux", "orb"),
        P(),
        P("orb", None),
        P("orb", None),
    )
    out_specs = P(("orb", "aux"), None)
    body = functools.partial(shards, mesh.shape["orb"], mesh.shape["aux"])
    return jax.shard_map(body, mesh=mesh, in_specs=in_specs, out_specs=out_specs, check_vma=False)
```

```python
import functools

import jax
import jax.numpy as jnp
from jax import lax
from jax.experimental import pallas as pl
from jax.experimental.pallas import tpu as pltpu
from jax.sharding import PartitionSpec as P

HIGHEST = lax.Precision.HIGHEST
HIGH = lax.Precision.HIGH
LANES = 128
TILE = 8
MIB = 1024 * 1024


def split(x):
    top = x.astype(jnp.bfloat16)
    return top, (x - top.astype(jnp.float32)).astype(jnp.bfloat16)


def mxu(a, b, contract):
    return lax.dot_general(a, b, (contract, ((), ())), preferred_element_type=jnp.float32)


def places():
    return tuple(pl.BlockSpec(memory_space=m) for m in (pltpu.SMEM, pltpu.VMEM, pltpu.HBM, pl.ANY))


def expand_mask(screen, half, chunk, rows):
    shells, blocks = screen.shape
    slab_rows = 2 * chunk // blocks
    row = lax.broadcasted_iota(jnp.int32, (chunk, blocks), 0) // slab_rows
    col = lax.broadcasted_iota(jnp.int32, (chunk, blocks), 1)
    down = (col == row + half * (blocks // 2)).astype(jnp.bfloat16)
    shell = lax.broadcasted_iota(jnp.int32, (shells, rows), 0)
    across = (shell == lax.broadcasted_iota(jnp.int32, (shells, rows), 1) // (rows // shells)).astype(jnp.bfloat16)
    tall = mxu(down, screen[...].astype(jnp.float32).astype(jnp.bfloat16), ((1,), (1,)))
    return mxu(tall.astype(jnp.bfloat16), across, ((1,), (0,)))


def extract_body(nb, info, active, three, screen, pairs, *refs):
    kept = refs[0]
    value, turned, found, mask, sem_in, sem_out, sem_kept = refs[-7:]
    act, parts, width = pairs.shape[1], pairs.shape[0], pairs.shape[3]
    _, chunk, rows = value.shape
    tiles = act // TILE
    start = pl.multiple_of(info[0] * chunk, chunk)

    def tile(i):
        return pl.ds(pl.multiple_of(i * TILE, TILE), TILE)

    def fetch(i):
        return pltpu.make_async_copy(three.at[tile(i), pl.ds(start, chunk), :], value.at[tile(i)], sem_in.at[i])

    def keep(i):
        return pltpu.make_async_copy(value.at[tile(i)], kept.at[tile(i)], sem_kept.at[i])

    for i in range(tiles):
        fetch(i).start()
    mask[...] = expand_mask(screen, info[0], chunk, rows)

    found[...] = jnp.zeros_like(found)

    @pl.loop(0, tiles)
    def _(i):
        fetch(i).wait()
        part = value[tile(i)] * mask[...][None]
        value[tile(i)] = part
        keep(i).start()
        for w in range(TILE):
            at = pl.ds(pl.multiple_of((i * TILE + w) * rows, rows), rows)
            for k in range(parts):
                turned[k, at, :] = part[w, k * width : (k + 1) * width].T

    @pl.loop(0, act // nb)
    def _(j):
        for t in range(nb):
            row = active[info[2 + j] * nb + t] - info[1]

            @pl.when(jnp.logical_and(row >= 0, row < rows))
            def _():
                for k in range(parts):
                    for i in range(tiles):
                        lines = turned[k, pl.ds(i * TILE * rows + row, TILE, stride=rows), :]
                        found[k, j * nb + t, i * TILE : (i + 1) * TILE, :] = lines

    give = pltpu.make_async_copy(found, pairs, sem_out)
    give.start()
    give.wait()
    for i in range(tiles):
        keep(i).wait()


def extract(three_index, screen_mask, active, info, chunk, width, nb):
    act, slab, rows = three_index.shape
    tiles = act // TILE
    out_shape = [
        jax.ShapeDtypeStruct((chunk // width, act, act, width), jnp.float32),
        jax.ShapeDtypeStruct((act, chunk, rows), jnp.float32),
    ]
    smem, vmem, hbm, anywhere = places()
    return pl.pallas_call(
        functools.partial(extract_body, nb),
        out_shape=out_shape,
        in_specs=[smem, smem, hbm, vmem],
        out_specs=[anywhere] * len(out_shape),
        scratch_shapes=[
            pltpu.VMEM((act, chunk, rows), jnp.float32),
            pltpu.VMEM((chunk // width, act * rows, width), jnp.float32),
            pltpu.VMEM((chunk // width, act, act, width), jnp.float32),
            pltpu.VMEM((chunk, rows), jnp.float32),
            pltpu.SemaphoreType.DMA((tiles,)),
            pltpu.SemaphoreType.DMA,
            pltpu.SemaphoreType.DMA((tiles,)),
        ],
        compiler_params=pltpu.CompilerParams(vmem_limit_bytes=50 * MIB),
        cost_estimate=pl.CostEstimate(
            flops=4 * act * act * chunk * rows,
            transcendentals=0,
            bytes_accessed=4 * act * chunk * (act + 2 * rows),
        ),
        name="extract",
    )(info, active, three_index, screen_mask)


def q_body(nb, count, info, kept, sib, *refs):
    blocks, (out, own, lhs, acc, sems) = refs[: 2 * count], refs[2 * count :]
    act, depth, rows = own.shape
    chunk = depth // 2
    height = acc.shape[0]

    def bring(tile, i):
        return pltpu.make_async_copy(kept.at[tile], own.at[tile], sems.at[i])

    for i in range(act // TILE):
        bring(pl.ds(i * TILE, TILE), i).start()
    lhs[...] = jnp.zeros_like(lhs)
    acc[...] = jnp.zeros_like(acc)
    nn = ((1,), (0,))

    @pl.loop(0, act // TILE)
    def _(i):
        tile = pl.ds(pl.multiple_of(i * TILE, TILE), TILE)
        for k in range(2):
            for j in range(count):
                for t in range(nb):
                    lhs[k, pl.ds(j * TILE + t, TILE, stride=height), :] = blocks[k * count + j][t, tile, :]
        pieces = [lhs[k, n * height : (n + 1) * height, :] for n in range(TILE) for k in range(2)]
        left, left_low = split(jnp.concatenate(pieces, axis=1))
        bring(tile, i).wait()
        right = [x[tile].reshape(TILE * depth, rows) for x in (own, sib)]
        top, low = split(jnp.concatenate(right, axis=1))
        both = mxu(jnp.concatenate([left, left_low], axis=0), top, nn)
        acc[...] += both[:height] + both[height:] + mxu(left, low, nn)

    for j in range(count):
        where = pl.multiple_of(info[2 + j] * TILE, TILE)
        out[pl.ds(where, TILE), :] = acc[j * TILE : (j + 1) * TILE, :]


def q_partial(own, sib, blocks, info):
    act, depth, rows = own.shape
    count = len(blocks[0])
    nb = act // count
    smem, vmem, hbm, anywhere = places()
    return pl.pallas_call(
        functools.partial(q_body, nb, count),
        out_shape=jax.ShapeDtypeStruct((count * TILE, 2 * rows), jnp.float32),
        in_specs=[smem, hbm, vmem] + [vmem] * (2 * count),
        out_specs=vmem,
        scratch_shapes=[
            pltpu.VMEM((act, depth, rows), jnp.float32),
            pltpu.VMEM((2, TILE * count * TILE, depth // 2), jnp.float32),
            pltpu.VMEM((count * TILE, 2 * rows), jnp.float32),
            pltpu.SemaphoreType.DMA((act // TILE,)),
        ],
        compiler_params=pltpu.CompilerParams(vmem_limit_bytes=49 * MIB),
        cost_estimate=pl.CostEstimate(
            flops=12 * act * act * depth * rows,
            transcendentals=0,
            bytes_accessed=4 * act * depth * (act + 2 * rows),
        ),
        name="qpartial",
    )(info, own, sib, *[b.reshape(nb, act, depth // 2) for half in blocks for b in half])


def half_body(chips, info, own, twin, *refs):
    count = 2 * (chips - 1)
    blocks, outs = refs[:count], refs[count : count + 2]
    held, acc = refs[count + 2 :]
    size, chunk = blocks[0].shape
    rows, depth = own.shape

    def place(hops):
        return pl.ds(pl.multiple_of(info[2 + hops] * size, TILE), size)

    for n in range(count):
        j, k = n // 2, n % 2
        held[place(j if j < chips // 2 else j + 1), k * chunk : (k + 1) * chunk] = blocks[n][...]
    held[place(chips // 2), :] = jnp.zeros((size, 2 * chunk), jnp.float32)
    acc[...] = jnp.zeros_like(acc)
    nn = ((1,), (0,))
    step = 6 * LANES

    def add(start, length):
        top, low = split(held[pl.ds(start, length), :])
        for h, density in enumerate((own, twin)):
            left, left_low = split(density[:, pl.ds(start, length)])
            acc[h] += mxu(left, top, nn) + mxu(left_low, top, nn) + mxu(left, low, nn)

    @pl.loop(0, depth // step)
    def _(i):
        add(pl.multiple_of(i * step, step), step)

    if depth % step:
        add(depth - depth % step, depth % step)
    core = info[2 + chips]
    for first in range(2):

        @pl.when(core == first)
        def _():
            for k in range(2):
                for h in range(2):
                    at = (h ^ first) * rows
                    outs[k][at : at + rows, :] = acc[h, :, k * chunk : (k + 1) * chunk]


def half_partial(own, twin, blocks, info, chips):
    size, chunk = blocks[0].shape
    rows, depth = own.shape
    smem, vmem, hbm, anywhere = places()
    return pl.pallas_call(
        functools.partial(half_body, chips),
        out_shape=[jax.ShapeDtypeStruct((2 * rows, chunk), jnp.float32)] * 2,
        in_specs=[smem, vmem, vmem] + [vmem] * len(blocks),
        out_specs=[vmem, vmem],
        scratch_shapes=[
            pltpu.VMEM((depth, 2 * chunk), jnp.float32),
            pltpu.VMEM((2, rows, 2 * chunk), jnp.float32),
        ],
        compiler_params=pltpu.CompilerParams(vmem_limit_bytes=14 * MIB),
        cost_estimate=pl.CostEstimate(
            flops=24 * rows * depth * chunk,
            transcendentals=0,
            bytes_accessed=8 * rows * depth + 8 * depth * chunk,
        ),
        name="half",
    )(info, own, twin, *blocks)


def fast(orb, aux, three_index, pair_density, active_orbitals, screen_mask, one_density, inactive_fock, active_fock):
    act, slab, rows = three_index.shape
    inactive = active_fock.shape[1]
    chips = orb // 2
    nb = act // chips
    blk = nb * act
    depth = slab // 2
    chunk = depth // 2
    me = lax.axis_index("orb")
    chip, core = lax.shift_right_logical(me, 1), lax.bitwise_and(me, 1)
    half_chip = lax.shift_right_logical(chip, 1)
    sign = 1 - 2 * core
    first_row = me * rows

    order = list(range(0, chips, 2)) + list(range(chips - 1, 0, -2))
    position = jnp.where(lax.bitwise_and(chip, 1) == 0, half_chip, chips - 1 - half_chip)

    def chip_at(sgn, hops):
        place = lax.rem(position + sgn * hops + chips, chips)
        return jnp.where(place < chips // 2, 2 * place, 2 * chips - 1 - 2 * place)

    def info_of(sgn, half):
        by_hops = chip_at(sgn, jnp.arange(chips, dtype=jnp.int32))
        return jnp.concatenate([jnp.stack([half, first_row]), by_hops, core.reshape(1)]).astype(jnp.int32)

    near = [(order[k], order[(k + 1) % chips]) for k in range(chips)]
    ahead = [(2 * a, 2 * b) for a, b in near] + [(2 * b + 1, 2 * a + 1) for a, b in near]
    behind = [(b, a) for a, b in ahead]
    twin = [(i, i ^ 1) for i in range(orb)]

    def hop(x, pairs):
        return lax.ppermute(x, "orb", pairs)

    local_rows = jnp.arange(rows, dtype=jnp.int32)
    mine, theirs = info_of(sign, core), info_of(-sign, 1 - core)

    shells = screen_mask.T
    far = chips // 2
    def pick(info):
        found, kept = extract(three_index, shells, active_orbitals, info, depth, chunk, nb)
        return found.reshape(2, act * act, chunk), kept

    other = hop(pair_density, twin)
    given, sib_three = pick(theirs)
    got = hop(given, twin)
    given, mine = lax.optimization_barrier((given, mine))
    found, own_three = pick(mine)
    contributions = []
    for k in range(2):
        contributions.append(
            [found[k, j * blk : (j + 1) * blk] + got[k, j * blk : (j + 1) * blk] for j in range(chips)]
        )
    inactive_fock, active_fock, contributions, other, sib_three = lax.optimization_barrier(
        (inactive_fock, active_fock, contributions, other, sib_three)
    )
    sib_three = hop(sib_three, twin)
    first = [(hop(c[far], ahead), hop(c[far + 1], behind)) for c in contributions]
    first, sib_three = lax.optimization_barrier((first, sib_three))
    totals = []
    for c, (a, b) in zip(contributions, first):
        for s in range(1, far):
            a = hop(a + c[far - s], ahead)
            if s < chips - 1 - far:
                b = hop(b + c[far + 1 + s], behind)
        totals.append(c[0] + a + b)
    totals = lax.optimization_barrier(totals)

    far_at = chip_at(sign, far) * blk
    far_columns = [lax.dynamic_slice_in_dim(d, far_at, blk, 1) for d in (pair_density, other)]
    density_far = jnp.concatenate(
        [jnp.where(core == 0, far_columns[0], far_columns[1]), jnp.where(core == 0, far_columns[1], far_columns[0])],
        axis=0,
    )

    def gather(x):
        blocks = [None] * chips
        blocks[0] = a = b = x
        for s in range(1, far + 1):
            a = hop(a, ahead)
            blocks[(chips - s) % chips] = a
            if s < chips - far:
                b = hop(b, behind)
                blocks[s] = b
        return blocks

    gathered = [gather(x) for x in totals]
    near_blocks = [gathered[k][j] for j in range(chips) if j != far for k in range(2)]
    halves = half_partial(pair_density, other, near_blocks, mine, chips)
    halves = [h + jnp.dot(density_far, gathered[k][far], precision=HIGH) for k, h in enumerate(halves)]
    halves = lax.optimization_barrier(halves)
    q = q_partial(own_three, sib_three, [gather(x) for x in halves], mine)
    q = q.reshape(chips, TILE, 2 * rows)[:, :nb].reshape(act, 2 * rows)

    share = rows // aux
    aux_at = lax.axis_index("aux")

    def across(x, orb_bits, aux_bits):
        table = [(o * aux + y, (o ^ orb_bits) * aux + (y ^ aux_bits)) for o in range(orb) for y in range(aux)]
        return lax.ppermute(x, ("orb", "aux"), table)

    closed = 2.0 * (inactive_fock[:, :inactive] + active_fock)
    opened = jnp.dot(inactive_fock[:, inactive:], one_density, precision=HIGHEST)
    closed_twin = hop(closed, twin)
    closed_chip = jnp.concatenate(
        [jnp.where(core == 0, closed, closed_twin), jnp.where(core == 0, closed_twin, closed)], axis=0
    )

    once = (aux_at == 0).astype(jnp.float32)
    own_q, twin_q = q[:, :rows] + once * opened.T, q[:, rows:]
    q_mine = own_q + hop(twin_q, twin)
    sent = lax.dynamic_slice_in_dim(q_mine, (1 - aux_at) * share, share, 1)
    q_rows = lax.dynamic_slice_in_dim(q_mine, aux_at * share, share, 1) + across(sent, 0, 1)

    occ_index = jnp.concatenate([jnp.arange(inactive, dtype=jnp.int32), active_orbitals])
    my_rows, twin_rows = first_row + local_rows, (me ^ 1) * rows + local_rows
    width = (inactive + act) // 2
    act_pick = (active_orbitals[:, None] == my_rows[None, :]).astype(jnp.float32) * once
    act_closed = jnp.pad(jnp.dot(act_pick, closed, precision=HIGHEST), ((0, 0), (0, act)))

    def picked(half):
        wanted = lax.dynamic_slice_in_dim(occ_index, half * width, width, 0)
        chosen = [(r[:, None] == wanted[None, :]).astype(jnp.float32) for r in (my_rows, twin_rows)]
        top = jnp.dot(jnp.concatenate([own_q, twin_q], axis=1), jnp.concatenate(chosen, axis=0), precision=HIGHEST)
        return jnp.concatenate([top, lax.dynamic_slice_in_dim(act_closed, half * width, width, 1)], axis=0)

    occ = picked(core) + hop(picked(1 - core), twin)
    occ = occ + across(occ, 2, 0) + across(occ, 0, 1) + across(occ, 2, 1)
    occ = occ + across(occ, 4, 0) + across(occ, 8, 0) + across(occ, 12, 0)
    occ_twin = hop(occ, twin)
    occ = jnp.concatenate([jnp.where(core == 0, occ, occ_twin), jnp.where(core == 0, occ_twin, occ)], axis=1)

    upper = jnp.concatenate([closed_chip[:inactive].T, occ[act:, :inactive].T], axis=1)
    occupied = jnp.concatenate([upper, occ[:act]], axis=0)

    mine_at = aux_at * share
    fock_mine = jnp.concatenate([lax.dynamic_slice_in_dim(closed, mine_at, share, 0), q_rows.T], axis=1)
    pick_rows = (first_row + mine_at + jnp.arange(share, dtype=jnp.int32))[:, None] == occ_index[None, :]
    transposed = jnp.dot(pick_rows.astype(jnp.float32), occupied, precision=HIGHEST)
    return 2.0 * (fock_mine - transposed)


def plain(orb, aux, three_index, pair_density, active_orbitals, screen_mask, one_density, inactive_fock, active_fock):
    act_count = three_index.shape[0]
    slab_count = three_index.shape[1]
    row_count = three_index.shape[2]
    inactive_count = active_fock.shape[1]
    orb_position = lax.axis_index("orb")
    kept_mask = jnp.repeat(
        jnp.repeat(screen_mask.astype(jnp.float32), slab_count // screen_mask.shape[0], axis=0),
        row_count // screen_mask.shape[1],
        axis=1,
    )
    screened = three_index * kept_mask[None]
    global_rows = orb_position * row_count + jnp.arange(row_count, dtype=jnp.int32)
    active_pick = (global_rows[:, None] == active_orbitals[None, :]).astype(jnp.float32)
    partial_pairs = jnp.einsum("wPp,pv->Pvw", screened, active_pick, precision=HIGHEST).reshape(
        slab_count, act_count * act_count
    )
    pairs = lax.psum(partial_pairs, "orb")
    column_block = jnp.dot(pairs, pair_density.T, precision=HIGHEST)
    half = lax.all_gather(column_block, "orb", axis=1, tiled=True)
    q_partial = jnp.einsum(
        "uPp,Ptu->pt", screened, half.reshape(slab_count, act_count, act_count), precision=HIGHEST
    )
    occ_index = jnp.concatenate([jnp.arange(inactive_count, dtype=jnp.int32), active_orbitals])
    row_share = row_count // aux
    aux_offset = lax.axis_index("aux") * row_share
    qmatrix = lax.psum(q_partial, "aux")
    inactive_cols = 2.0 * (inactive_fock[:, :inactive_count] + active_fock)
    active_cols = jnp.dot(inactive_fock[:, inactive_count:], one_density, precision=HIGHEST) + qmatrix
    fock = jnp.concatenate([inactive_cols, active_cols], axis=1)
    occ_pick = (global_rows[:, None] == occ_index[None, :]).astype(jnp.float32)
    occupied = lax.psum(jnp.dot(occ_pick.T, fock, precision=HIGHEST), "orb")
    fock_mine = lax.dynamic_slice_in_dim(fock, aux_offset, row_share, 0)
    pick_mine = lax.dynamic_slice_in_dim(occ_pick, aux_offset, row_share, 0)
    transposed = jnp.dot(pick_mine, occupied.T, precision=HIGHEST)
    return 2.0 * (fock_mine - transposed)


def shards(orb, aux, *args):
    act, slab, rows = args[0].shape
    chips = orb // 2
    fits = orb == 16 and aux == 2 and act % chips == 0 and act % TILE == 0
    fits = fits and args[6].shape[1] <= 2 * rows and (args[6].shape[1] + act) % 2 == 0
    fits = fits and slab % (4 * LANES) == 0 and rows % LANES == 0
    return (fast if fits else plain)(orb, aux, *args)


def solution(mesh):
    in_specs = (
        P(None, "aux", "orb"),
        P("orb", None),
        P(),
        P("aux", "orb"),
        P(),
        P("orb", None),
        P("orb", None),
    )
    out_specs = P(("orb", "aux"), None)
    body = functools.partial(shards, mesh.shape["orb"], mesh.shape["aux"])
    return jax.shard_map(body, mesh=mesh, in_specs=in_specs, out_specs=out_specs, check_vma=False)
```

```python
import functools

import jax
import jax.numpy as jnp
from jax import lax
from jax.experimental import pallas as pl
from jax.experimental.pallas import tpu as pltpu
from jax.sharding import PartitionSpec as P

HIGHEST = lax.Precision.HIGHEST
HIGH = lax.Precision.HIGH
LANES = 128
TILE = 8
MIB = 1024 * 1024


def split(x):
    top = x.astype(jnp.bfloat16)
    return top, (x - top.astype(jnp.float32)).astype(jnp.bfloat16)


def mxu(a, b, contract):
    return lax.dot_general(a, b, (contract, ((), ())), preferred_element_type=jnp.float32)


def places():
    return tuple(pl.BlockSpec(memory_space=m) for m in (pltpu.SMEM, pltpu.VMEM, pltpu.HBM, pl.ANY))


def expand_mask(screen, half, chunk, rows):
    shells, blocks = screen.shape
    slab_rows = 2 * chunk // blocks
    row = lax.broadcasted_iota(jnp.int32, (chunk, blocks), 0) // slab_rows
    col = lax.broadcasted_iota(jnp.int32, (chunk, blocks), 1)
    down = (col == row + half * (blocks // 2)).astype(jnp.bfloat16)
    shell = lax.broadcasted_iota(jnp.int32, (shells, rows), 0)
    across = (shell == lax.broadcasted_iota(jnp.int32, (shells, rows), 1) // (rows // shells)).astype(jnp.bfloat16)
    tall = mxu(down, screen[...].astype(jnp.float32).astype(jnp.bfloat16), ((1,), (1,)))
    return mxu(tall.astype(jnp.bfloat16), across, ((1,), (0,)))


def extract_body(nb, parts, info, active, three, screen, *refs):
    pairs, kept = refs[:parts], refs[parts] if len(refs) == parts + 8 else None
    value, turned, found, mask, sem_in, sem_out, sem_kept = refs[-7:]
    act, _, width = pairs[0].shape
    _, chunk, rows = value.shape
    tiles = act // TILE
    start = pl.multiple_of(info[0] * chunk, chunk)

    def tile(i):
        return pl.ds(pl.multiple_of(i * TILE, TILE), TILE)

    def fetch(i):
        return pltpu.make_async_copy(three.at[tile(i), pl.ds(start, chunk), :], value.at[tile(i)], sem_in.at[i])

    def keep(i):
        return pltpu.make_async_copy(value.at[tile(i)], kept.at[tile(i)], sem_kept.at[i])

    for i in range(tiles):
        fetch(i).start()
    mask[...] = expand_mask(screen, info[0], chunk, rows)

    found[...] = jnp.zeros_like(found)

    @pl.loop(0, tiles)
    def _(i):
        fetch(i).wait()
        part = value[tile(i)] * mask[...][None]
        if kept is not None:
            value[tile(i)] = part
            keep(i).start()
        for w in range(TILE):
            at = pl.ds(pl.multiple_of((i * TILE + w) * rows, rows), rows)
            for k in range(parts):
                turned[k, at, :] = part[w, k * width : (k + 1) * width].T

    @pl.loop(0, act // nb)
    def _(j):
        for t in range(nb):
            row = active[info[2 + j] * nb + t] - info[1]

            @pl.when(jnp.logical_and(row >= 0, row < rows))
            def _():
                for k in range(parts):
                    for i in range(tiles):
                        lines = turned[k, pl.ds(i * TILE * rows + row, TILE, stride=rows), :]
                        found[k, j * nb + t, i * TILE : (i + 1) * TILE, :] = lines

    def give(k):
        return pltpu.make_async_copy(found.at[k], pairs[k], sem_out.at[k])

    for k in range(parts):
        give(k).start()
    for k in range(parts):
        give(k).wait()
    if kept is not None:
        for i in range(tiles):
            keep(i).wait()


def extract(three_index, screen_mask, active, info, chunk, width, nb, keep):
    act, slab, rows = three_index.shape
    tiles = act // TILE
    parts = chunk // width
    out_shape = [jax.ShapeDtypeStruct((act, act, width), jnp.float32)] * parts
    if keep:
        out_shape.append(jax.ShapeDtypeStruct((act, chunk, rows), jnp.float32))
    smem, vmem, hbm, anywhere = places()
    return pl.pallas_call(
        functools.partial(extract_body, nb, parts),
        out_shape=out_shape,
        in_specs=[smem, smem, hbm, vmem],
        out_specs=[anywhere] * len(out_shape),
        scratch_shapes=[
            pltpu.VMEM((act, chunk, rows), jnp.float32),
            pltpu.VMEM((chunk // width, act * rows, width), jnp.float32),
            pltpu.VMEM((chunk // width, act, act, width), jnp.float32),
            pltpu.VMEM((chunk, rows), jnp.float32),
            pltpu.SemaphoreType.DMA((tiles,)),
            pltpu.SemaphoreType.DMA((parts,)),
            pltpu.SemaphoreType.DMA((tiles,)),
        ],
        compiler_params=pltpu.CompilerParams(vmem_limit_bytes=50 * MIB),
        cost_estimate=pl.CostEstimate(
            flops=4 * act * act * chunk * rows,
            transcendentals=0,
            bytes_accessed=4 * act * chunk * (act + rows * (2 if keep else 1)),
        ),
        name="extract",
    )(info, active, three_index, screen_mask)


def q_body(nb, count, info, three, screen, sib, *refs):
    blocks, (out, own, lhs, acc, mask, sems) = refs[: 2 * count], refs[2 * count :]
    act, depth, rows = own.shape
    chunk = depth // 2
    height = acc.shape[0]

    start = pl.multiple_of(info[0] * depth, depth)

    def bring(tile, i):
        return pltpu.make_async_copy(three.at[tile, pl.ds(start, depth), :], own.at[tile], sems.at[i])

    for i in range(act // TILE):
        bring(pl.ds(i * TILE, TILE), i).start()
    mask[...] = expand_mask(screen, info[0], depth, rows)
    lhs[...] = jnp.zeros_like(lhs)
    acc[...] = jnp.zeros_like(acc)
    nn = ((1,), (0,))

    @pl.loop(0, act // TILE)
    def _(i):
        tile = pl.ds(pl.multiple_of(i * TILE, TILE), TILE)
        for k in range(2):
            for j in range(count):
                for t in range(nb):
                    lhs[k, pl.ds(j * TILE + t, TILE, stride=height), :] = blocks[k * count + j][t, tile, :]
        pieces = [lhs[k, n * height : (n + 1) * height, :] for n in range(TILE) for k in range(2)]
        left, left_low = split(jnp.concatenate(pieces, axis=1))
        bring(tile, i).wait()
        right = [x.reshape(TILE * depth, rows) for x in (own[tile] * mask[...][None], sib[tile])]
        top, low = split(jnp.concatenate(right, axis=1))
        both = mxu(jnp.concatenate([left, left_low], axis=0), top, nn)
        acc[...] += both[:height] + both[height:] + mxu(left, low, nn)

    for j in range(count):
        where = pl.multiple_of(info[2 + j] * TILE, TILE)
        out[pl.ds(where, TILE), :] = acc[j * TILE : (j + 1) * TILE, :]


def q_partial(three_index, screen_mask, sib, blocks, info):
    act, depth, rows = sib.shape
    count = len(blocks[0])
    nb = act // count
    smem, vmem, hbm, anywhere = places()
    return pl.pallas_call(
        functools.partial(q_body, nb, count),
        out_shape=jax.ShapeDtypeStruct((count * TILE, 2 * rows), jnp.float32),
        in_specs=[smem, hbm, vmem, vmem] + [vmem] * (2 * count),
        out_specs=vmem,
        scratch_shapes=[
            pltpu.VMEM((act, depth, rows), jnp.float32),
            pltpu.VMEM((2, TILE * count * TILE, depth // 2), jnp.float32),
            pltpu.VMEM((count * TILE, 2 * rows), jnp.float32),
            pltpu.VMEM((depth, rows), jnp.float32),
            pltpu.SemaphoreType.DMA((act // TILE,)),
        ],
        compiler_params=pltpu.CompilerParams(vmem_limit_bytes=49 * MIB),
        cost_estimate=pl.CostEstimate(
            flops=12 * act * act * depth * rows,
            transcendentals=0,
            bytes_accessed=4 * act * depth * (act + 2 * rows),
        ),
        name="qpartial",
    )(info, three_index, screen_mask, sib, *[b.reshape(nb, act, depth // 2) for half in blocks for b in half])


def half_body(chips, info, own, twin, *refs):
    count = 2 * (chips - 1)
    blocks, outs = refs[:count], refs[count : count + 2]
    held, acc = refs[count + 2 :]
    size, chunk = blocks[0].shape
    rows, depth = own.shape

    def place(hops):
        return pl.ds(pl.multiple_of(info[2 + hops] * size, TILE), size)

    for n in range(count):
        j, k = n // 2, n % 2
        held[place(j if j < chips // 2 else j + 1), k * chunk : (k + 1) * chunk] = blocks[n][...]
    held[place(chips // 2), :] = jnp.zeros((size, 2 * chunk), jnp.float32)
    acc[...] = jnp.zeros_like(acc)
    nn = ((1,), (0,))
    step = 6 * LANES

    def add(start, length):
        top, low = split(held[pl.ds(start, length), :])
        for h, density in enumerate((own, twin)):
            left, left_low = split(density[:, pl.ds(start, length)])
            acc[h] += mxu(left, top, nn) + mxu(left_low, top, nn) + mxu(left, low, nn)

    @pl.loop(0, depth // step)
    def _(i):
        add(pl.multiple_of(i * step, step), step)

    if depth % step:
        add(depth - depth % step, depth % step)
    core = info[2 + chips]
    for first in range(2):

        @pl.when(core == first)
        def _():
            for k in range(2):
                for h in range(2):
                    at = (h ^ first) * rows
                    outs[k][at : at + rows, :] = acc[h, :, k * chunk : (k + 1) * chunk]


def half_partial(own, twin, blocks, info, chips):
    size, chunk = blocks[0].shape
    rows, depth = own.shape
    smem, vmem, hbm, anywhere = places()
    return pl.pallas_call(
        functools.partial(half_body, chips),
        out_shape=[jax.ShapeDtypeStruct((2 * rows, chunk), jnp.float32)] * 2,
        in_specs=[smem, vmem, vmem] + [vmem] * len(blocks),
        out_specs=[vmem, vmem],
        scratch_shapes=[
            pltpu.VMEM((depth, 2 * chunk), jnp.float32),
            pltpu.VMEM((2, rows, 2 * chunk), jnp.float32),
        ],
        compiler_params=pltpu.CompilerParams(vmem_limit_bytes=14 * MIB),
        cost_estimate=pl.CostEstimate(
            flops=24 * rows * depth * chunk,
            transcendentals=0,
            bytes_accessed=8 * rows * depth + 8 * depth * chunk,
        ),
        name="half",
    )(info, own, twin, *blocks)


def fast(orb, aux, three_index, pair_density, active_orbitals, screen_mask, one_density, inactive_fock, active_fock):
    act, slab, rows = three_index.shape
    inactive = active_fock.shape[1]
    chips = orb // 2
    nb = act // chips
    blk = nb * act
    depth = slab // 2
    chunk = depth // 2
    me = lax.axis_index("orb")
    chip, core = lax.shift_right_logical(me, 1), lax.bitwise_and(me, 1)
    half_chip = lax.shift_right_logical(chip, 1)
    sign = 1 - 2 * core
    first_row = me * rows

    order = list(range(0, chips, 2)) + list(range(chips - 1, 0, -2))
    position = jnp.where(lax.bitwise_and(chip, 1) == 0, half_chip, chips - 1 - half_chip)

    def chip_at(sgn, hops):
        place = lax.rem(position + sgn * hops + chips, chips)
        return jnp.where(place < chips // 2, 2 * place, 2 * chips - 1 - 2 * place)

    def info_of(sgn, half):
        by_hops = chip_at(sgn, jnp.arange(chips, dtype=jnp.int32))
        return jnp.concatenate([jnp.stack([half, first_row]), by_hops, core.reshape(1)]).astype(jnp.int32)

    near = [(order[k], order[(k + 1) % chips]) for k in range(chips)]
    ahead = [(2 * a, 2 * b) for a, b in near] + [(2 * b + 1, 2 * a + 1) for a, b in near]
    behind = [(b, a) for a, b in ahead]
    twin = [(i, i ^ 1) for i in range(orb)]

    def hop(x, pairs):
        return lax.ppermute(x, "orb", pairs)

    local_rows = jnp.arange(rows, dtype=jnp.int32)
    mine, theirs = info_of(sign, core), info_of(-sign, 1 - core)

    shells = screen_mask.T
    far = chips // 2
    def pick(info, keep):
        *found, last = extract(three_index, shells, active_orbitals, info, depth, chunk, nb, keep)
        flat = [f.reshape(act * act, chunk) for f in (found if keep else found + [last])]
        return flat, last

    other = hop(pair_density, twin)
    given, sib_three = pick(theirs, True)
    got = [hop(g, twin) for g in given]
    given, mine = lax.optimization_barrier((given, mine))
    found, _ = pick(mine, False)
    contributions = []
    for f, g in zip(found, got):
        contributions.append([f[j * blk : (j + 1) * blk] + g[j * blk : (j + 1) * blk] for j in range(chips)])
    inactive_fock, active_fock, contributions, other, sib_three = lax.optimization_barrier(
        (inactive_fock, active_fock, contributions, other, sib_three)
    )
    sib_three = hop(sib_three, twin)
    first = [(hop(c[far], ahead), hop(c[far + 1], behind)) for c in contributions]
    first, sib_three = lax.optimization_barrier((first, sib_three))
    totals = []
    for c, (a, b) in zip(contributions, first):
        for s in range(1, far):
            a = hop(a + c[far - s], ahead)
            if s < chips - 1 - far:
                b = hop(b + c[far + 1 + s], behind)
        totals.append(c[0] + a + b)
    totals = lax.optimization_barrier(totals)

    far_at = chip_at(sign, far) * blk
    far_columns = [lax.dynamic_slice_in_dim(d, far_at, blk, 1) for d in (pair_density, other)]
    density_far = jnp.concatenate(
        [jnp.where(core == 0, far_columns[0], far_columns[1]), jnp.where(core == 0, far_columns[1], far_columns[0])],
        axis=0,
    )

    def gather(x):
        blocks = [None] * chips
        blocks[0] = a = b = x
        for s in range(1, far + 1):
            a = hop(a, ahead)
            blocks[(chips - s) % chips] = a
            if s < chips - far:
                b = hop(b, behind)
                blocks[s] = b
        return blocks

    gathered = [gather(x) for x in totals]
    near_blocks = [gathered[k][j] for j in range(chips) if j != far for k in range(2)]
    halves = half_partial(pair_density, other, near_blocks, mine, chips)
    halves = [h + jnp.dot(density_far, gathered[k][far], precision=HIGH) for k, h in enumerate(halves)]
    halves = lax.optimization_barrier(halves)
    q = q_partial(three_index, shells, sib_three, [gather(x) for x in halves], mine)
    q = q.reshape(chips, TILE, 2 * rows)[:, :nb].reshape(act, 2 * rows)

    share = rows // aux
    aux_at = lax.axis_index("aux")

    def across(x, orb_bits, aux_bits):
        table = [(o * aux + y, (o ^ orb_bits) * aux + (y ^ aux_bits)) for o in range(orb) for y in range(aux)]
        return lax.ppermute(x, ("orb", "aux"), table)

    closed = 2.0 * (inactive_fock[:, :inactive] + active_fock)
    opened = jnp.dot(inactive_fock[:, inactive:], one_density, precision=HIGHEST)
    closed_twin = hop(closed, twin)
    closed_chip = jnp.concatenate(
        [jnp.where(core == 0, closed, closed_twin), jnp.where(core == 0, closed_twin, closed)], axis=0
    )

    once = (aux_at == 0).astype(jnp.float32)
    own_q, twin_q = q[:, :rows] + once * opened.T, q[:, rows:]
    occ_index = jnp.concatenate([jnp.arange(inactive, dtype=jnp.int32), active_orbitals])
    my_rows, twin_rows = first_row + local_rows, (me ^ 1) * rows + local_rows
    width = (inactive + act) // 2
    act_pick = (active_orbitals[:, None] == my_rows[None, :]).astype(jnp.float32) * once
    act_closed = jnp.pad(jnp.dot(act_pick, closed, precision=HIGHEST), ((0, 0), (0, act)))

    def picked(half):
        wanted = lax.dynamic_slice_in_dim(occ_index, half * width, width, 0)
        chosen = [(r[:, None] == wanted[None, :]).astype(jnp.float32) for r in (my_rows, twin_rows)]
        top = jnp.dot(jnp.concatenate([own_q, twin_q], axis=1), jnp.concatenate(chosen, axis=0), precision=HIGHEST)
        return jnp.concatenate([top, lax.dynamic_slice_in_dim(act_closed, half * width, width, 1)], axis=0)

    keep_occ, send_occ = picked(core), picked(1 - core)
    twin_q, keep_occ, send_occ = lax.optimization_barrier((twin_q, keep_occ, send_occ))
    occ = keep_occ + hop(send_occ, twin)

    q_mine = own_q + hop(twin_q, twin)
    sent = lax.dynamic_slice_in_dim(q_mine, (1 - aux_at) * share, share, 1)
    q_rows = lax.dynamic_slice_in_dim(q_mine, aux_at * share, share, 1) + across(sent, 0, 1)

    occ = occ + across(occ, 2, 0) + across(occ, 0, 1) + across(occ, 2, 1)
    occ = occ + across(occ, 4, 0) + across(occ, 8, 0) + across(occ, 12, 0)
    occ_twin = hop(occ, twin)
    occ = jnp.concatenate([jnp.where(core == 0, occ, occ_twin), jnp.where(core == 0, occ_twin, occ)], axis=1)

    upper = jnp.concatenate([closed_chip[:inactive].T, occ[act:, :inactive].T], axis=1)
    occupied = jnp.concatenate([upper, occ[:act]], axis=0)

    mine_at = aux_at * share
    fock_mine = jnp.concatenate([lax.dynamic_slice_in_dim(closed, mine_at, share, 0), q_rows.T], axis=1)
    pick_rows = (first_row + mine_at + jnp.arange(share, dtype=jnp.int32))[:, None] == occ_index[None, :]
    transposed = jnp.dot(pick_rows.astype(jnp.float32), occupied, precision=HIGHEST)
    return 2.0 * (fock_mine - transposed)


def plain(orb, aux, three_index, pair_density, active_orbitals, screen_mask, one_density, inactive_fock, active_fock):
    act_count = three_index.shape[0]
    slab_count = three_index.shape[1]
    row_count = three_index.shape[2]
    inactive_count = active_fock.shape[1]
    orb_position = lax.axis_index("orb")
    kept_mask = jnp.repeat(
        jnp.repeat(screen_mask.astype(jnp.float32), slab_count // screen_mask.shape[0], axis=0),
        row_count // screen_mask.shape[1],
        axis=1,
    )
    screened = three_index * kept_mask[None]
    global_rows = orb_position * row_count + jnp.arange(row_count, dtype=jnp.int32)
    active_pick = (global_rows[:, None] == active_orbitals[None, :]).astype(jnp.float32)
    partial_pairs = jnp.einsum("wPp,pv->Pvw", screened, active_pick, precision=HIGHEST).reshape(
        slab_count, act_count * act_count
    )
    pairs = lax.psum(partial_pairs, "orb")
    column_block = jnp.dot(pairs, pair_density.T, precision=HIGHEST)
    half = lax.all_gather(column_block, "orb", axis=1, tiled=True)
    q_partial = jnp.einsum(
        "uPp,Ptu->pt", screened, half.reshape(slab_count, act_count, act_count), precision=HIGHEST
    )
    occ_index = jnp.concatenate([jnp.arange(inactive_count, dtype=jnp.int32), active_orbitals])
    row_share = row_count // aux
    aux_offset = lax.axis_index("aux") * row_share
    qmatrix = lax.psum(q_partial, "aux")
    inactive_cols = 2.0 * (inactive_fock[:, :inactive_count] + active_fock)
    active_cols = jnp.dot(inactive_fock[:, inactive_count:], one_density, precision=HIGHEST) + qmatrix
    fock = jnp.concatenate([inactive_cols, active_cols], axis=1)
    occ_pick = (global_rows[:, None] == occ_index[None, :]).astype(jnp.float32)
    occupied = lax.psum(jnp.dot(occ_pick.T, fock, precision=HIGHEST), "orb")
    fock_mine = lax.dynamic_slice_in_dim(fock, aux_offset, row_share, 0)
    pick_mine = lax.dynamic_slice_in_dim(occ_pick, aux_offset, row_share, 0)
    transposed = jnp.dot(pick_mine, occupied.T, precision=HIGHEST)
    return 2.0 * (fock_mine - transposed)


def shards(orb, aux, *args):
    act, slab, rows = args[0].shape
    chips = orb // 2
    fits = orb == 16 and aux == 2 and act % chips == 0 and act % TILE == 0
    fits = fits and args[6].shape[1] <= 2 * rows and (args[6].shape[1] + act) % 2 == 0
    fits = fits and slab % (4 * LANES) == 0 and rows % LANES == 0
    return (fast if fits else plain)(orb, aux, *args)


def solution(mesh):
    in_specs = (
        P(None, "aux", "orb"),
        P("orb", None),
        P(),
        P("aux", "orb"),
        P(),
        P("orb", None),
        P("orb", None),
    )
    out_specs = P(("orb", "aux"), None)
    body = functools.partial(shards, mesh.shape["orb"], mesh.shape["aux"])
    return jax.shard_map(body, mesh=mesh, in_specs=in_specs, out_specs=out_specs, check_vma=False)
```

```python
import functools

import jax
import jax.numpy as jnp
from jax import lax
from jax.experimental import pallas as pl
from jax.experimental.pallas import tpu as pltpu
from jax.sharding import PartitionSpec as P

HIGHEST = lax.Precision.HIGHEST
HIGH = lax.Precision.HIGH
LANES = 128
TILE = 8
MIB = 1024 * 1024


def split(x):
    top = x.astype(jnp.bfloat16)
    return top, (x - top.astype(jnp.float32)).astype(jnp.bfloat16)


def mxu(a, b, contract):
    return lax.dot_general(a, b, (contract, ((), ())), preferred_element_type=jnp.float32)


def places():
    return tuple(pl.BlockSpec(memory_space=m) for m in (pltpu.SMEM, pltpu.VMEM, pltpu.HBM, pl.ANY))


def expand_mask(screen, half, chunk, rows):
    shells, blocks = screen.shape
    slab_rows = 2 * chunk // blocks
    row = lax.broadcasted_iota(jnp.int32, (chunk, blocks), 0) // slab_rows
    col = lax.broadcasted_iota(jnp.int32, (chunk, blocks), 1)
    down = (col == row + half * (blocks // 2)).astype(jnp.bfloat16)
    shell = lax.broadcasted_iota(jnp.int32, (shells, rows), 0)
    across = (shell == lax.broadcasted_iota(jnp.int32, (shells, rows), 1) // (rows // shells)).astype(jnp.bfloat16)
    tall = mxu(down, screen[...].astype(jnp.float32).astype(jnp.bfloat16), ((1,), (1,)))
    return mxu(tall.astype(jnp.bfloat16), across, ((1,), (0,)))


def extract_body(nb, parts, info, active, three, screen, *refs):
    pairs, kept = refs[:parts], refs[parts] if len(refs) == parts + 8 else None
    value, turned, found, mask, sem_in, sem_out, sem_kept = refs[-7:]
    act, _, width = pairs[0].shape
    _, chunk, rows = value.shape
    tiles = act // TILE
    start = pl.multiple_of(info[0] * chunk, chunk)

    def tile(i):
        return pl.ds(pl.multiple_of(i * TILE, TILE), TILE)

    def fetch(i):
        return pltpu.make_async_copy(three.at[tile(i), pl.ds(start, chunk), :], value.at[tile(i)], sem_in.at[i])

    def keep(i):
        return pltpu.make_async_copy(value.at[tile(i)], kept.at[tile(i)], sem_kept.at[i])

    for i in range(tiles):
        fetch(i).start()
    mask[...] = expand_mask(screen, info[0], chunk, rows)

    found[...] = jnp.zeros_like(found)

    @pl.loop(0, tiles)
    def _(i):
        fetch(i).wait()
        part = value[tile(i)] * mask[...][None]
        if kept is not None:
            value[tile(i)] = part
            keep(i).start()
        for w in range(TILE):
            at = pl.ds(pl.multiple_of((i * TILE + w) * rows, rows), rows)
            for k in range(parts):
                turned[k, at, :] = part[w, k * width : (k + 1) * width].T

    @pl.loop(0, act // nb)
    def _(j):
        for t in range(nb):
            row = active[info[2 + j] * nb + t] - info[1]

            @pl.when(jnp.logical_and(row >= 0, row < rows))
            def _():
                for k in range(parts):
                    for i in range(tiles):
                        lines = turned[k, pl.ds(i * TILE * rows + row, TILE, stride=rows), :]
                        found[k, j * nb + t, i * TILE : (i + 1) * TILE, :] = lines

    def give(k):
        return pltpu.make_async_copy(found.at[k], pairs[k], sem_out.at[k])

    for k in range(parts):
        give(k).start()
    for k in range(parts):
        give(k).wait()
    if kept is not None:
        for i in range(tiles):
            keep(i).wait()


def extract(three_index, screen_mask, active, info, chunk, width, nb, keep):
    act, slab, rows = three_index.shape
    tiles = act // TILE
    parts = chunk // width
    out_shape = [jax.ShapeDtypeStruct((act, act, width), jnp.float32)] * parts
    if keep:
        out_shape.append(jax.ShapeDtypeStruct((act, chunk, rows), jnp.float32))
    smem, vmem, hbm, anywhere = places()
    return pl.pallas_call(
        functools.partial(extract_body, nb, parts),
        out_shape=out_shape,
        in_specs=[smem, smem, hbm, vmem],
        out_specs=[anywhere] * len(out_shape),
        scratch_shapes=[
            pltpu.VMEM((act, chunk, rows), jnp.float32),
            pltpu.VMEM((chunk // width, act * rows, width), jnp.float32),
            pltpu.VMEM((chunk // width, act, act, width), jnp.float32),
            pltpu.VMEM((chunk, rows), jnp.float32),
            pltpu.SemaphoreType.DMA((tiles,)),
            pltpu.SemaphoreType.DMA((parts,)),
            pltpu.SemaphoreType.DMA((tiles,)),
        ],
        compiler_params=pltpu.CompilerParams(vmem_limit_bytes=50 * MIB),
        cost_estimate=pl.CostEstimate(
            flops=4 * act * act * chunk * rows,
            transcendentals=0,
            bytes_accessed=4 * act * chunk * (act + rows * (2 if keep else 1)),
        ),
        name="extract",
    )(info, active, three_index, screen_mask)


def q_body(nb, count, info, three, screen, sib, *refs):
    blocks, (out, own, lhs, acc, mask, sems) = refs[: 2 * count], refs[2 * count :]
    act, depth, rows = own.shape
    chunk = depth // 2
    height = acc.shape[0]

    start = pl.multiple_of(info[0] * depth, depth)

    def bring(tile, i):
        return pltpu.make_async_copy(three.at[tile, pl.ds(start, depth), :], own.at[tile], sems.at[i])

    for i in range(act // TILE):
        bring(pl.ds(i * TILE, TILE), i).start()
    mask[...] = expand_mask(screen, info[0], depth, rows)
    lhs[...] = jnp.zeros_like(lhs)
    acc[...] = jnp.zeros_like(acc)
    nn = ((1,), (0,))

    @pl.loop(0, act // TILE)
    def _(i):
        tile = pl.ds(pl.multiple_of(i * TILE, TILE), TILE)
        for k in range(2):
            for j in range(count):
                for t in range(nb):
                    lhs[k, pl.ds(j * TILE + t, TILE, stride=height), :] = blocks[k * count + j][t, tile, :]
        pieces = [lhs[k, n * height : (n + 1) * height, :] for n in range(TILE) for k in range(2)]
        left, left_low = split(jnp.concatenate(pieces, axis=1))
        bring(tile, i).wait()
        right = [x.reshape(TILE * depth, rows) for x in (own[tile] * mask[...][None], sib[tile])]
        top, low = split(jnp.concatenate(right, axis=1))
        both = mxu(jnp.concatenate([left, left_low], axis=0), top, nn)
        acc[...] += both[:height] + both[height:] + mxu(left, low, nn)

    for j in range(count):
        where = pl.multiple_of(info[2 + j] * TILE, TILE)
        out[pl.ds(where, TILE), :] = acc[j * TILE : (j + 1) * TILE, :]


def q_partial(three_index, screen_mask, sib, blocks, info):
    act, depth, rows = sib.shape
    count = len(blocks[0])
    nb = act // count
    smem, vmem, hbm, anywhere = places()
    return pl.pallas_call(
        functools.partial(q_body, nb, count),
        out_shape=jax.ShapeDtypeStruct((count * TILE, 2 * rows), jnp.float32),
        in_specs=[smem, hbm, vmem, vmem] + [vmem] * (2 * count),
        out_specs=vmem,
        scratch_shapes=[
            pltpu.VMEM((act, depth, rows), jnp.float32),
            pltpu.VMEM((2, TILE * count * TILE, depth // 2), jnp.float32),
            pltpu.VMEM((count * TILE, 2 * rows), jnp.float32),
            pltpu.VMEM((depth, rows), jnp.float32),
            pltpu.SemaphoreType.DMA((act // TILE,)),
        ],
        compiler_params=pltpu.CompilerParams(vmem_limit_bytes=49 * MIB),
        cost_estimate=pl.CostEstimate(
            flops=12 * act * act * depth * rows,
            transcendentals=0,
            bytes_accessed=4 * act * depth * (act + 2 * rows),
        ),
        name="qpartial",
    )(info, three_index, screen_mask, sib, *[b.reshape(nb, act, depth // 2) for half in blocks for b in half])


def half_body(chips, info, own, twin, *refs):
    count = 2 * (chips - 1)
    blocks, outs = refs[:count], refs[count : count + 2]
    held, acc = refs[count + 2 :]
    size, chunk = blocks[0].shape
    rows, depth = own.shape

    def place(hops):
        return pl.ds(pl.multiple_of(info[2 + hops] * size, TILE), size)

    for n in range(count):
        j, k = n // 2, n % 2
        held[place(j if j < chips // 2 else j + 1), k * chunk : (k + 1) * chunk] = blocks[n][...]
    held[place(chips // 2), :] = jnp.zeros((size, 2 * chunk), jnp.float32)
    acc[...] = jnp.zeros_like(acc)
    nn = ((1,), (0,))
    step = 6 * LANES

    def add(start, length):
        top, low = split(held[pl.ds(start, length), :])
        for h, density in enumerate((own, twin)):
            left, left_low = split(density[:, pl.ds(start, length)])
            acc[h] += mxu(left, top, nn) + mxu(left_low, top, nn) + mxu(left, low, nn)

    @pl.loop(0, depth // step, unroll=True)
    def _(i):
        add(pl.multiple_of(i * step, step), step)

    if depth % step:
        add(depth - depth % step, depth % step)
    core = info[2 + chips]
    for first in range(2):

        @pl.when(core == first)
        def _():
            for k in range(2):
                for h in range(2):
                    at = (h ^ first) * rows
                    outs[k][at : at + rows, :] = acc[h, :, k * chunk : (k + 1) * chunk]


def half_partial(own, twin, blocks, info, chips):
    size, chunk = blocks[0].shape
    rows, depth = own.shape
    smem, vmem, hbm, anywhere = places()
    return pl.pallas_call(
        functools.partial(half_body, chips),
        out_shape=[jax.ShapeDtypeStruct((2 * rows, chunk), jnp.float32)] * 2,
        in_specs=[smem, vmem, vmem] + [vmem] * len(blocks),
        out_specs=[vmem, vmem],
        scratch_shapes=[
            pltpu.VMEM((depth, 2 * chunk), jnp.float32),
            pltpu.VMEM((2, rows, 2 * chunk), jnp.float32),
        ],
        compiler_params=pltpu.CompilerParams(vmem_limit_bytes=14 * MIB),
        cost_estimate=pl.CostEstimate(
            flops=24 * rows * depth * chunk,
            transcendentals=0,
            bytes_accessed=8 * rows * depth + 8 * depth * chunk,
        ),
        name="half",
    )(info, own, twin, *blocks)


def fast(orb, aux, three_index, pair_density, active_orbitals, screen_mask, one_density, inactive_fock, active_fock):
    act, slab, rows = three_index.shape
    inactive = active_fock.shape[1]
    chips = orb // 2
    nb = act // chips
    blk = nb * act
    depth = slab // 2
    chunk = depth // 2
    me = lax.axis_index("orb")
    chip, core = lax.shift_right_logical(me, 1), lax.bitwise_and(me, 1)
    half_chip = lax.shift_right_logical(chip, 1)
    sign = 1 - 2 * core
    first_row = me * rows

    order = list(range(0, chips, 2)) + list(range(chips - 1, 0, -2))
    position = jnp.where(lax.bitwise_and(chip, 1) == 0, half_chip, chips - 1 - half_chip)

    def chip_at(sgn, hops):
        place = lax.rem(position + sgn * hops + chips, chips)
        return jnp.where(place < chips // 2, 2 * place, 2 * chips - 1 - 2 * place)

    def info_of(sgn, half):
        by_hops = chip_at(sgn, jnp.arange(chips, dtype=jnp.int32))
        return jnp.concatenate([jnp.stack([half, first_row]), by_hops, core.reshape(1)]).astype(jnp.int32)

    near = [(order[k], order[(k + 1) % chips]) for k in range(chips)]
    ahead = [(2 * a, 2 * b) for a, b in near] + [(2 * b + 1, 2 * a + 1) for a, b in near]
    behind = [(b, a) for a, b in ahead]
    twin = [(i, i ^ 1) for i in range(orb)]

    def hop(x, pairs):
        return lax.ppermute(x, "orb", pairs)

    local_rows = jnp.arange(rows, dtype=jnp.int32)
    mine, theirs = info_of(sign, core), info_of(-sign, 1 - core)

    shells = screen_mask.T
    far = chips // 2
    def pick(info, keep):
        *found, last = extract(three_index, shells, active_orbitals, info, depth, chunk, nb, keep)
        flat = [f.reshape(act * act, chunk) for f in (found if keep else found + [last])]
        return flat, last

    other = hop(pair_density, twin)
    given, sib_three = pick(theirs, True)
    got = [hop(g, twin) for g in given]
    given, mine = lax.optimization_barrier((given, mine))
    found, _ = pick(mine, False)
    contributions = []
    for f, g in zip(found, got):
        contributions.append([f[j * blk : (j + 1) * blk] + g[j * blk : (j + 1) * blk] for j in range(chips)])
    inactive_fock, active_fock, contributions, other, sib_three = lax.optimization_barrier(
        (inactive_fock, active_fock, contributions, other, sib_three)
    )
    sib_three = hop(sib_three, twin)
    first = [(hop(c[far], ahead), hop(c[far + 1], behind)) for c in contributions]
    first, sib_three = lax.optimization_barrier((first, sib_three))
    totals = []
    for c, (a, b) in zip(contributions, first):
        for s in range(1, far):
            a = hop(a + c[far - s], ahead)
            if s < chips - 1 - far:
                b = hop(b + c[far + 1 + s], behind)
        totals.append(c[0] + a + b)
    totals = lax.optimization_barrier(totals)

    far_at = chip_at(sign, far) * blk
    far_columns = [lax.dynamic_slice_in_dim(d, far_at, blk, 1) for d in (pair_density, other)]
    density_far = jnp.concatenate(
        [jnp.where(core == 0, far_columns[0], far_columns[1]), jnp.where(core == 0, far_columns[1], far_columns[0])],
        axis=0,
    )

    def gather(x):
        blocks = [None] * chips
        blocks[0] = a = b = x
        for s in range(1, far + 1):
            a = hop(a, ahead)
            blocks[(chips - s) % chips] = a
            if s < chips - far:
                b = hop(b, behind)
                blocks[s] = b
        return blocks

    gathered = [gather(x) for x in totals]
    near_blocks = [gathered[k][j] for j in range(chips) if j != far for k in range(2)]
    halves = half_partial(pair_density, other, near_blocks, mine, chips)
    halves = [h + jnp.dot(density_far, gathered[k][far], precision=HIGH) for k, h in enumerate(halves)]
    halves = lax.optimization_barrier(halves)
    q = q_partial(three_index, shells, sib_three, [gather(x) for x in halves], mine)
    q = q.reshape(chips, TILE, 2 * rows)[:, :nb].reshape(act, 2 * rows)

    share = rows // aux
    aux_at = lax.axis_index("aux")

    def across(x, orb_bits, aux_bits):
        table = [(o * aux + y, (o ^ orb_bits) * aux + (y ^ aux_bits)) for o in range(orb) for y in range(aux)]
        return lax.ppermute(x, ("orb", "aux"), table)

    closed = 2.0 * (inactive_fock[:, :inactive] + active_fock)
    opened = jnp.dot(inactive_fock[:, inactive:], one_density, precision=HIGHEST)
    closed_twin = hop(closed, twin)
    closed_chip = jnp.concatenate(
        [jnp.where(core == 0, closed, closed_twin), jnp.where(core == 0, closed_twin, closed)], axis=0
    )

    once = (aux_at == 0).astype(jnp.float32)
    own_q, twin_q = q[:, :rows] + once * opened.T, q[:, rows:]
    occ_index = jnp.concatenate([jnp.arange(inactive, dtype=jnp.int32), active_orbitals])
    my_rows, twin_rows = first_row + local_rows, (me ^ 1) * rows + local_rows
    width = (inactive + act) // 2
    act_pick = (active_orbitals[:, None] == my_rows[None, :]).astype(jnp.float32) * once
    act_closed = jnp.pad(jnp.dot(act_pick, closed, precision=HIGHEST), ((0, 0), (0, act)))

    def picked(half):
        wanted = lax.dynamic_slice_in_dim(occ_index, half * width, width, 0)
        chosen = [(r[:, None] == wanted[None, :]).astype(jnp.float32) for r in (my_rows, twin_rows)]
        top = jnp.dot(jnp.concatenate([own_q, twin_q], axis=1), jnp.concatenate(chosen, axis=0), precision=HIGHEST)
        return jnp.concatenate([top, lax.dynamic_slice_in_dim(act_closed, half * width, width, 1)], axis=0)

    keep_occ, send_occ = picked(core), picked(1 - core)
    twin_q, keep_occ, send_occ = lax.optimization_barrier((twin_q, keep_occ, send_occ))
    occ = keep_occ + hop(send_occ, twin)

    q_mine = own_q + hop(twin_q, twin)
    sent = lax.dynamic_slice_in_dim(q_mine, (1 - aux_at) * share, share, 1)
    q_rows = lax.dynamic_slice_in_dim(q_mine, aux_at * share, share, 1) + across(sent, 0, 1)

    occ = occ + across(occ, 2, 0) + across(occ, 0, 1) + across(occ, 2, 1)
    occ = occ + across(occ, 4, 0) + across(occ, 8, 0) + across(occ, 12, 0)
    occ_twin = hop(occ, twin)
    occ = jnp.concatenate([jnp.where(core == 0, occ, occ_twin), jnp.where(core == 0, occ_twin, occ)], axis=1)

    upper = jnp.concatenate([closed_chip[:inactive].T, occ[act:, :inactive].T], axis=1)
    occupied = jnp.concatenate([upper, occ[:act]], axis=0)

    mine_at = aux_at * share
    fock_mine = jnp.concatenate([lax.dynamic_slice_in_dim(closed, mine_at, share, 0), q_rows.T], axis=1)
    pick_rows = (first_row + mine_at + jnp.arange(share, dtype=jnp.int32))[:, None] == occ_index[None, :]
    transposed = jnp.dot(pick_rows.astype(jnp.float32), occupied, precision=HIGHEST)
    return 2.0 * (fock_mine - transposed)


def plain(orb, aux, three_index, pair_density, active_orbitals, screen_mask, one_density, inactive_fock, active_fock):
    act_count = three_index.shape[0]
    slab_count = three_index.shape[1]
    row_count = three_index.shape[2]
    inactive_count = active_fock.shape[1]
    orb_position = lax.axis_index("orb")
    kept_mask = jnp.repeat(
        jnp.repeat(screen_mask.astype(jnp.float32), slab_count // screen_mask.shape[0], axis=0),
        row_count // screen_mask.shape[1],
        axis=1,
    )
    screened = three_index * kept_mask[None]
    global_rows = orb_position * row_count + jnp.arange(row_count, dtype=jnp.int32)
    active_pick = (global_rows[:, None] == active_orbitals[None, :]).astype(jnp.float32)
    partial_pairs = jnp.einsum("wPp,pv->Pvw", screened, active_pick, precision=HIGHEST).reshape(
        slab_count, act_count * act_count
    )
    pairs = lax.psum(partial_pairs, "orb")
    column_block = jnp.dot(pairs, pair_density.T, precision=HIGHEST)
    half = lax.all_gather(column_block, "orb", axis=1, tiled=True)
    q_partial = jnp.einsum(
        "uPp,Ptu->pt", screened, half.reshape(slab_count, act_count, act_count), precision=HIGHEST
    )
    occ_index = jnp.concatenate([jnp.arange(inactive_count, dtype=jnp.int32), active_orbitals])
    row_share = row_count // aux
    aux_offset = lax.axis_index("aux") * row_share
    qmatrix = lax.psum(q_partial, "aux")
    inactive_cols = 2.0 * (inactive_fock[:, :inactive_count] + active_fock)
    active_cols = jnp.dot(inactive_fock[:, inactive_count:], one_density, precision=HIGHEST) + qmatrix
    fock = jnp.concatenate([inactive_cols, active_cols], axis=1)
    occ_pick = (global_rows[:, None] == occ_index[None, :]).astype(jnp.float32)
    occupied = lax.psum(jnp.dot(occ_pick.T, fock, precision=HIGHEST), "orb")
    fock_mine = lax.dynamic_slice_in_dim(fock, aux_offset, row_share, 0)
    pick_mine = lax.dynamic_slice_in_dim(occ_pick, aux_offset, row_share, 0)
    transposed = jnp.dot(pick_mine, occupied.T, precision=HIGHEST)
    return 2.0 * (fock_mine - transposed)


def shards(orb, aux, *args):
    act, slab, rows = args[0].shape
    chips = orb // 2
    fits = orb == 16 and aux == 2 and act % chips == 0 and act % TILE == 0
    fits = fits and args[6].shape[1] <= 2 * rows and (args[6].shape[1] + act) % 2 == 0
    fits = fits and slab % (4 * LANES) == 0 and rows % LANES == 0
    return (fast if fits else plain)(orb, aux, *args)


def solution(mesh):
    in_specs = (
        P(None, "aux", "orb"),
        P("orb", None),
        P(),
        P("aux", "orb"),
        P(),
        P("orb", None),
        P("orb", None),
    )
    out_specs = P(("orb", "aux"), None)
    body = functools.partial(shards, mesh.shape["orb"], mesh.shape["aux"])
    return jax.shard_map(body, mesh=mesh, in_specs=in_specs, out_specs=out_specs, check_vma=False)
```

```python
import functools

import jax
import jax.numpy as jnp
from jax import lax
from jax.experimental import pallas as pl
from jax.experimental.pallas import tpu as pltpu
from jax.sharding import PartitionSpec as P

HIGHEST = lax.Precision.HIGHEST
HIGH = lax.Precision.HIGH
LANES = 128
TILE = 8
MIB = 1024 * 1024


def split(x):
    top = x.astype(jnp.bfloat16)
    return top, (x - top.astype(jnp.float32)).astype(jnp.bfloat16)


def mxu(a, b, contract):
    return lax.dot_general(a, b, (contract, ((), ())), preferred_element_type=jnp.float32)


def places():
    return tuple(pl.BlockSpec(memory_space=m) for m in (pltpu.SMEM, pltpu.VMEM, pltpu.HBM, pl.ANY))


def expand_mask(screen, half, chunk, rows):
    shells, blocks = screen.shape
    slab_rows = 2 * chunk // blocks
    row = lax.broadcasted_iota(jnp.int32, (chunk, blocks), 0) // slab_rows
    col = lax.broadcasted_iota(jnp.int32, (chunk, blocks), 1)
    down = (col == row + half * (blocks // 2)).astype(jnp.bfloat16)
    shell = lax.broadcasted_iota(jnp.int32, (shells, rows), 0)
    across = (shell == lax.broadcasted_iota(jnp.int32, (shells, rows), 1) // (rows // shells)).astype(jnp.bfloat16)
    tall = mxu(down, screen[...].astype(jnp.float32).astype(jnp.bfloat16), ((1,), (1,)))
    return mxu(tall.astype(jnp.bfloat16), across, ((1,), (0,)))


def extract_body(nb, parts, info, active, three, screen, *refs):
    pairs, kept = refs[:parts], refs[parts] if len(refs) == parts + 8 else None
    value, turned, found, mask, sem_in, sem_out, sem_kept = refs[-7:]
    act, _, width = pairs[0].shape
    _, chunk, rows = value.shape
    tiles = act // TILE
    start = pl.multiple_of(info[0] * chunk, chunk)

    def tile(i):
        return pl.ds(pl.multiple_of(i * TILE, TILE), TILE)

    def fetch(i):
        return pltpu.make_async_copy(three.at[tile(i), pl.ds(start, chunk), :], value.at[tile(i)], sem_in.at[i])

    def keep(i):
        return pltpu.make_async_copy(value.at[tile(i)], kept.at[tile(i)], sem_kept.at[i])

    for i in range(tiles):
        fetch(i).start()
    mask[...] = expand_mask(screen, info[0], chunk, rows)

    found[...] = jnp.zeros_like(found)

    @pl.loop(0, tiles)
    def _(i):
        fetch(i).wait()
        part = value[tile(i)] * mask[...][None]
        if kept is not None:
            value[tile(i)] = part
            keep(i).start()
        for w in range(TILE):
            at = pl.ds(pl.multiple_of((i * TILE + w) * rows, rows), rows)
            for k in range(parts):
                turned[k, at, :] = part[w, k * width : (k + 1) * width].T

    @pl.loop(0, act // nb)
    def _(j):
        for t in range(nb):
            row = active[info[2 + j] * nb + t] - info[1]

            @pl.when(jnp.logical_and(row >= 0, row < rows))
            def _():
                for k in range(parts):
                    for i in range(tiles):
                        lines = turned[k, pl.ds(i * TILE * rows + row, TILE, stride=rows), :]
                        found[k, j * nb + t, i * TILE : (i + 1) * TILE, :] = lines

    def give(k):
        return pltpu.make_async_copy(found.at[k], pairs[k], sem_out.at[k])

    for k in range(parts):
        give(k).start()
    for k in range(parts):
        give(k).wait()
    if kept is not None:
        for i in range(tiles):
            keep(i).wait()


def extract(three_index, screen_mask, active, info, chunk, width, nb, keep):
    act, slab, rows = three_index.shape
    tiles = act // TILE
    parts = chunk // width
    out_shape = [jax.ShapeDtypeStruct((act, act, width), jnp.float32)] * parts
    if keep:
        out_shape.append(jax.ShapeDtypeStruct((act, chunk, rows), jnp.float32))
    smem, vmem, hbm, anywhere = places()
    return pl.pallas_call(
        functools.partial(extract_body, nb, parts),
        out_shape=out_shape,
        in_specs=[smem, smem, hbm, vmem],
        out_specs=[anywhere] * len(out_shape),
        scratch_shapes=[
            pltpu.VMEM((act, chunk, rows), jnp.float32),
            pltpu.VMEM((chunk // width, act * rows, width), jnp.float32),
            pltpu.VMEM((chunk // width, act, act, width), jnp.float32),
            pltpu.VMEM((chunk, rows), jnp.float32),
            pltpu.SemaphoreType.DMA((tiles,)),
            pltpu.SemaphoreType.DMA((parts,)),
            pltpu.SemaphoreType.DMA((tiles,)),
        ],
        compiler_params=pltpu.CompilerParams(vmem_limit_bytes=50 * MIB),
        cost_estimate=pl.CostEstimate(
            flops=4 * act * act * chunk * rows,
            transcendentals=0,
            bytes_accessed=4 * act * chunk * (act + rows * (2 if keep else 1)),
        ),
        name="extract",
    )(info, active, three_index, screen_mask)


def q_body(nb, count, info, three, screen, sib, *refs):
    blocks, (out, own, lhs, acc, mask, sems) = refs[: 2 * count], refs[2 * count :]
    act, depth, rows = own.shape
    chunk = depth // 2
    height = acc.shape[0]

    start = pl.multiple_of(info[0] * depth, depth)

    def bring(tile, i):
        return pltpu.make_async_copy(three.at[tile, pl.ds(start, depth), :], own.at[tile], sems.at[i])

    for i in range(act // TILE):
        bring(pl.ds(i * TILE, TILE), i).start()
    mask[...] = expand_mask(screen, info[0], depth, rows)
    lhs[...] = jnp.zeros_like(lhs)
    acc[...] = jnp.zeros_like(acc)
    nn = ((1,), (0,))

    @pl.loop(0, act // TILE)
    def _(i):
        tile = pl.ds(pl.multiple_of(i * TILE, TILE), TILE)
        for k in range(2):
            for j in range(count):
                for t in range(nb):
                    lhs[k, pl.ds(j * TILE + t, TILE, stride=height), :] = blocks[k * count + j][t, tile, :]
        pieces = [lhs[k, n * height : (n + 1) * height, :] for n in range(TILE) for k in range(2)]
        left, left_low = split(jnp.concatenate(pieces, axis=1))
        bring(tile, i).wait()
        right = [x.reshape(TILE * depth, rows) for x in (own[tile] * mask[...][None], sib[tile])]
        top, low = split(jnp.concatenate(right, axis=1))
        both = mxu(jnp.concatenate([left, left_low], axis=0), top, nn)
        acc[...] += both[:height] + both[height:] + mxu(left, low, nn)

    for j in range(count):
        where = pl.multiple_of(info[2 + j] * TILE, TILE)
        out[pl.ds(where, TILE), :] = acc[j * TILE : (j + 1) * TILE, :]


def q_partial(three_index, screen_mask, sib, blocks, info):
    act, depth, rows = sib.shape
    count = len(blocks[0])
    nb = act // count
    smem, vmem, hbm, anywhere = places()
    return pl.pallas_call(
        functools.partial(q_body, nb, count),
        out_shape=jax.ShapeDtypeStruct((count * TILE, 2 * rows), jnp.float32),
        in_specs=[smem, hbm, vmem, vmem] + [vmem] * (2 * count),
        out_specs=vmem,
        scratch_shapes=[
            pltpu.VMEM((act, depth, rows), jnp.float32),
            pltpu.VMEM((2, TILE * count * TILE, depth // 2), jnp.float32),
            pltpu.VMEM((count * TILE, 2 * rows), jnp.float32),
            pltpu.VMEM((depth, rows), jnp.float32),
            pltpu.SemaphoreType.DMA((act // TILE,)),
        ],
        compiler_params=pltpu.CompilerParams(vmem_limit_bytes=49 * MIB),
        cost_estimate=pl.CostEstimate(
            flops=12 * act * act * depth * rows,
            transcendentals=0,
            bytes_accessed=4 * act * depth * (act + 2 * rows),
        ),
        name="qpartial",
    )(info, three_index, screen_mask, sib, *[b.reshape(nb, act, depth // 2) for half in blocks for b in half])


def half_body(chips, info, own, twin, *refs):
    count = 2 * (chips - 1)
    blocks, outs = refs[:count], refs[count : count + 2]
    held, acc = refs[count + 2 :]
    size, chunk = blocks[0].shape
    rows, depth = own.shape

    def place(hops):
        return pl.ds(pl.multiple_of(info[2 + hops] * size, TILE), size)

    for n in range(count):
        j, k = n // 2, n % 2
        held[place(j if j < chips // 2 else j + 1), k * chunk : (k + 1) * chunk] = blocks[n][...]
    held[place(chips // 2), :] = jnp.zeros((size, 2 * chunk), jnp.float32)
    acc[...] = jnp.zeros_like(acc)
    nn = ((1,), (0,))
    step = 6 * LANES

    def add(start, length):
        top, low = split(held[pl.ds(start, length), :])
        for h, density in enumerate((own, twin)):
            left, left_low = split(density[:, pl.ds(start, length)])
            acc[h] += mxu(left, top, nn) + mxu(left_low, top, nn) + mxu(left, low, nn)

    @pl.loop(0, depth // step, unroll=True)
    def _(i):
        add(pl.multiple_of(i * step, step), step)

    if depth % step:
        add(depth - depth % step, depth % step)
    core = info[2 + chips]
    for first in range(2):

        @pl.when(core == first)
        def _():
            for k in range(2):
                for h in range(2):
                    at = (h ^ first) * rows
                    outs[k][at : at + rows, :] = acc[h, :, k * chunk : (k + 1) * chunk]


def half_partial(own, twin, blocks, info, chips):
    size, chunk = blocks[0].shape
    rows, depth = own.shape
    smem, vmem, hbm, anywhere = places()
    return pl.pallas_call(
        functools.partial(half_body, chips),
        out_shape=[jax.ShapeDtypeStruct((2 * rows, chunk), jnp.float32)] * 2,
        in_specs=[smem, vmem, vmem] + [vmem] * len(blocks),
        out_specs=[vmem, vmem],
        scratch_shapes=[
            pltpu.VMEM((depth, 2 * chunk), jnp.float32),
            pltpu.VMEM((2, rows, 2 * chunk), jnp.float32),
        ],
        compiler_params=pltpu.CompilerParams(vmem_limit_bytes=14 * MIB),
        cost_estimate=pl.CostEstimate(
            flops=24 * rows * depth * chunk,
            transcendentals=0,
            bytes_accessed=8 * rows * depth + 8 * depth * chunk,
        ),
        name="half",
    )(info, own, twin, *blocks)


def fast(orb, aux, three_index, pair_density, active_orbitals, screen_mask, one_density, inactive_fock, active_fock):
    act, slab, rows = three_index.shape
    inactive = active_fock.shape[1]
    chips = orb // 2
    nb = act // chips
    blk = nb * act
    depth = slab // 2
    chunk = depth // 2
    me = lax.axis_index("orb")
    chip, core = lax.shift_right_logical(me, 1), lax.bitwise_and(me, 1)
    half_chip = lax.shift_right_logical(chip, 1)
    sign = 1 - 2 * core
    first_row = me * rows

    order = list(range(0, chips, 2)) + list(range(chips - 1, 0, -2))
    position = jnp.where(lax.bitwise_and(chip, 1) == 0, half_chip, chips - 1 - half_chip)

    def chip_at(sgn, hops):
        place = lax.rem(position + sgn * hops + chips, chips)
        return jnp.where(place < chips // 2, 2 * place, 2 * chips - 1 - 2 * place)

    def info_of(sgn, half):
        by_hops = chip_at(sgn, jnp.arange(chips, dtype=jnp.int32))
        return jnp.concatenate([jnp.stack([half, first_row]), by_hops, core.reshape(1)]).astype(jnp.int32)

    near = [(order[k], order[(k + 1) % chips]) for k in range(chips)]
    ahead = [(2 * a, 2 * b) for a, b in near] + [(2 * b + 1, 2 * a + 1) for a, b in near]
    behind = [(b, a) for a, b in ahead]
    twin = [(i, i ^ 1) for i in range(orb)]

    def hop(x, pairs):
        return lax.ppermute(x, "orb", pairs)

    local_rows = jnp.arange(rows, dtype=jnp.int32)
    mine, theirs = info_of(sign, core), info_of(-sign, 1 - core)

    shells = screen_mask.T
    far = chips // 2
    def pick(info, keep):
        *found, last = extract(three_index, shells, active_orbitals, info, depth, chunk, nb, keep)
        flat = [f.reshape(act * act, chunk) for f in (found if keep else found + [last])]
        return flat, last

    other = hop(pair_density, twin)
    given, sib_three = pick(theirs, True)
    got = [hop(g, twin) for g in given]
    given, mine = lax.optimization_barrier((given, mine))
    found, _ = pick(mine, False)
    contributions = []
    for f, g in zip(found, got):
        contributions.append([f[j * blk : (j + 1) * blk] + g[j * blk : (j + 1) * blk] for j in range(chips)])
    inactive_fock, active_fock, contributions, other, sib_three = lax.optimization_barrier(
        (inactive_fock, active_fock, contributions, other, sib_three)
    )
    sib_three = hop(sib_three, twin)
    first = [(hop(c[far], ahead), hop(c[far + 1], behind)) for c in contributions]
    first, sib_three = lax.optimization_barrier((first, sib_three))
    totals = []
    for c, (a, b) in zip(contributions, first):
        for s in range(1, far):
            a = hop(a + c[far - s], ahead)
            if s < chips - 1 - far:
                b = hop(b + c[far + 1 + s], behind)
        totals.append(c[0] + a + b)

    far_at = chip_at(sign, far) * blk
    far_columns = [lax.dynamic_slice_in_dim(d, far_at, blk, 1) for d in (pair_density, other)]
    density_far = jnp.concatenate(
        [jnp.where(core == 0, far_columns[0], far_columns[1]), jnp.where(core == 0, far_columns[1], far_columns[0])],
        axis=0,
    )

    def gather(x):
        blocks = [None] * chips
        blocks[0] = a = b = x
        for s in range(1, far + 1):
            a = hop(a, ahead)
            blocks[(chips - s) % chips] = a
            if s < chips - far:
                b = hop(b, behind)
                blocks[s] = b
        return blocks

    gathered = [gather(x) for x in totals]
    near_blocks = [gathered[k][j] for j in range(chips) if j != far for k in range(2)]
    halves = half_partial(pair_density, other, near_blocks, mine, chips)
    halves = [h + jnp.dot(density_far, gathered[k][far], precision=HIGH) for k, h in enumerate(halves)]
    halves = lax.optimization_barrier(halves)
    q = q_partial(three_index, shells, sib_three, [gather(x) for x in halves], mine)
    q = q.reshape(chips, TILE, 2 * rows)[:, :nb].reshape(act, 2 * rows)

    share = rows // aux
    aux_at = lax.axis_index("aux")

    def across(x, orb_bits, aux_bits):
        table = [(o * aux + y, (o ^ orb_bits) * aux + (y ^ aux_bits)) for o in range(orb) for y in range(aux)]
        return lax.ppermute(x, ("orb", "aux"), table)

    closed = 2.0 * (inactive_fock[:, :inactive] + active_fock)
    opened = jnp.dot(inactive_fock[:, inactive:], one_density, precision=HIGHEST)
    closed_twin = hop(closed, twin)
    closed_chip = jnp.concatenate(
        [jnp.where(core == 0, closed, closed_twin), jnp.where(core == 0, closed_twin, closed)], axis=0
    )

    once = (aux_at == 0).astype(jnp.float32)
    own_q, twin_q = q[:, :rows] + once * opened.T, q[:, rows:]
    occ_index = jnp.concatenate([jnp.arange(inactive, dtype=jnp.int32), active_orbitals])
    my_rows, twin_rows = first_row + local_rows, (me ^ 1) * rows + local_rows
    width = (inactive + act) // 2
    act_pick = (active_orbitals[:, None] == my_rows[None, :]).astype(jnp.float32) * once
    act_closed = jnp.pad(jnp.dot(act_pick, closed, precision=HIGHEST), ((0, 0), (0, act)))

    def picked(half):
        wanted = lax.dynamic_slice_in_dim(occ_index, half * width, width, 0)
        chosen = [(r[:, None] == wanted[None, :]).astype(jnp.float32) for r in (my_rows, twin_rows)]
        top = jnp.dot(jnp.concatenate([own_q, twin_q], axis=1), jnp.concatenate(chosen, axis=0), precision=HIGHEST)
        return jnp.concatenate([top, lax.dynamic_slice_in_dim(act_closed, half * width, width, 1)], axis=0)

    keep_occ, send_occ = picked(core), picked(1 - core)
    twin_q, keep_occ, send_occ = lax.optimization_barrier((twin_q, keep_occ, send_occ))
    occ = keep_occ + hop(send_occ, twin)

    q_mine = own_q + hop(twin_q, twin)
    sent = lax.dynamic_slice_in_dim(q_mine, (1 - aux_at) * share, share, 1)
    q_rows = lax.dynamic_slice_in_dim(q_mine, aux_at * share, share, 1) + across(sent, 0, 1)

    occ = occ + across(occ, 2, 0) + across(occ, 0, 1) + across(occ, 2, 1)
    occ = occ + across(occ, 4, 0) + across(occ, 8, 0) + across(occ, 12, 0)
    occ_twin = hop(occ, twin)
    occ = jnp.concatenate([jnp.where(core == 0, occ, occ_twin), jnp.where(core == 0, occ_twin, occ)], axis=1)

    upper = jnp.concatenate([closed_chip[:inactive].T, occ[act:, :inactive].T], axis=1)
    occupied = jnp.concatenate([upper, occ[:act]], axis=0)

    mine_at = aux_at * share
    fock_mine = jnp.concatenate([lax.dynamic_slice_in_dim(closed, mine_at, share, 0), q_rows.T], axis=1)
    pick_rows = (first_row + mine_at + jnp.arange(share, dtype=jnp.int32))[:, None] == occ_index[None, :]
    transposed = jnp.dot(pick_rows.astype(jnp.float32), occupied, precision=HIGHEST)
    return 2.0 * (fock_mine - transposed)


def plain(orb, aux, three_index, pair_density, active_orbitals, screen_mask, one_density, inactive_fock, active_fock):
    act_count = three_index.shape[0]
    slab_count = three_index.shape[1]
    row_count = three_index.shape[2]
    inactive_count = active_fock.shape[1]
    orb_position = lax.axis_index("orb")
    kept_mask = jnp.repeat(
        jnp.repeat(screen_mask.astype(jnp.float32), slab_count // screen_mask.shape[0], axis=0),
        row_count // screen_mask.shape[1],
        axis=1,
    )
    screened = three_index * kept_mask[None]
    global_rows = orb_position * row_count + jnp.arange(row_count, dtype=jnp.int32)
    active_pick = (global_rows[:, None] == active_orbitals[None, :]).astype(jnp.float32)
    partial_pairs = jnp.einsum("wPp,pv->Pvw", screened, active_pick, precision=HIGHEST).reshape(
        slab_count, act_count * act_count
    )
    pairs = lax.psum(partial_pairs, "orb")
    column_block = jnp.dot(pairs, pair_density.T, precision=HIGHEST)
    half = lax.all_gather(column_block, "orb", axis=1, tiled=True)
    q_partial = jnp.einsum(
        "uPp,Ptu->pt", screened, half.reshape(slab_count, act_count, act_count), precision=HIGHEST
    )
    occ_index = jnp.concatenate([jnp.arange(inactive_count, dtype=jnp.int32), active_orbitals])
    row_share = row_count // aux
    aux_offset = lax.axis_index("aux") * row_share
    qmatrix = lax.psum(q_partial, "aux")
    inactive_cols = 2.0 * (inactive_fock[:, :inactive_count] + active_fock)
    active_cols = jnp.dot(inactive_fock[:, inactive_count:], one_density, precision=HIGHEST) + qmatrix
    fock = jnp.concatenate([inactive_cols, active_cols], axis=1)
    occ_pick = (global_rows[:, None] == occ_index[None, :]).astype(jnp.float32)
    occupied = lax.psum(jnp.dot(occ_pick.T, fock, precision=HIGHEST), "orb")
    fock_mine = lax.dynamic_slice_in_dim(fock, aux_offset, row_share, 0)
    pick_mine = lax.dynamic_slice_in_dim(occ_pick, aux_offset, row_share, 0)
    transposed = jnp.dot(pick_mine, occupied.T, precision=HIGHEST)
    return 2.0 * (fock_mine - transposed)


def shards(orb, aux, *args):
    act, slab, rows = args[0].shape
    chips = orb // 2
    fits = orb == 16 and aux == 2 and act % chips == 0 and act % TILE == 0
    fits = fits and args[6].shape[1] <= 2 * rows and (args[6].shape[1] + act) % 2 == 0
    fits = fits and slab % (4 * LANES) == 0 and rows % LANES == 0
    return (fast if fits else plain)(orb, aux, *args)


def solution(mesh):
    in_specs = (
        P(None, "aux", "orb"),
        P("orb", None),
        P(),
        P("aux", "orb"),
        P(),
        P("orb", None),
        P("orb", None),
    )
    out_specs = P(("orb", "aux"), None)
    body = functools.partial(shards, mesh.shape["orb"], mesh.shape["aux"])
    return jax.shard_map(body, mesh=mesh, in_specs=in_specs, out_specs=out_specs, check_vma=False)
```

```python
import functools

import jax
import jax.numpy as jnp
from jax import lax
from jax.experimental import pallas as pl
from jax.experimental.pallas import tpu as pltpu
from jax.sharding import PartitionSpec as P

HIGHEST = lax.Precision.HIGHEST
HIGH = lax.Precision.HIGH
LANES = 128
TILE = 8
MIB = 1024 * 1024


def split(x):
    top = x.astype(jnp.bfloat16)
    return top, (x - top.astype(jnp.float32)).astype(jnp.bfloat16)


def mxu(a, b, contract):
    return lax.dot_general(a, b, (contract, ((), ())), preferred_element_type=jnp.float32)


def places():
    return tuple(pl.BlockSpec(memory_space=m) for m in (pltpu.SMEM, pltpu.VMEM, pltpu.HBM, pl.ANY))


def expand_mask(screen, half, chunk, rows):
    shells, blocks = screen.shape
    slab_rows = 2 * chunk // blocks
    row = lax.broadcasted_iota(jnp.int32, (chunk, blocks), 0) // slab_rows
    col = lax.broadcasted_iota(jnp.int32, (chunk, blocks), 1)
    down = (col == row + half * (blocks // 2)).astype(jnp.bfloat16)
    shell = lax.broadcasted_iota(jnp.int32, (shells, rows), 0)
    across = (shell == lax.broadcasted_iota(jnp.int32, (shells, rows), 1) // (rows // shells)).astype(jnp.bfloat16)
    tall = mxu(down, screen[...].astype(jnp.float32).astype(jnp.bfloat16), ((1,), (1,)))
    return mxu(tall.astype(jnp.bfloat16), across, ((1,), (0,)))


def extract_body(nb, parts, info, active, three, screen, *refs):
    pairs, kept = refs[:parts], refs[parts] if len(refs) == parts + 8 else None
    value, turned, found, mask, sem_in, sem_out, sem_kept = refs[-7:]
    act, _, width = pairs[0].shape
    _, chunk, rows = value.shape
    tiles = act // TILE
    start = pl.multiple_of(info[0] * chunk, chunk)

    def tile(i):
        return pl.ds(pl.multiple_of(i * TILE, TILE), TILE)

    def fetch(i):
        return pltpu.make_async_copy(three.at[tile(i), pl.ds(start, chunk), :], value.at[tile(i)], sem_in.at[i])

    def keep(i):
        return pltpu.make_async_copy(value.at[tile(i)], kept.at[tile(i)], sem_kept.at[i])

    for i in range(tiles):
        fetch(i).start()
    mask[...] = expand_mask(screen, info[0], chunk, rows)

    found[...] = jnp.zeros_like(found)

    @pl.loop(0, tiles)
    def _(i):
        fetch(i).wait()
        part = value[tile(i)] * mask[...][None]
        if kept is not None:
            value[tile(i)] = part
            keep(i).start()
        for w in range(TILE):
            at = pl.ds(pl.multiple_of((i * TILE + w) * rows, rows), rows)
            for k in range(parts):
                turned[k, at, :] = part[w, k * width : (k + 1) * width].T

    @pl.loop(0, act // nb)
    def _(j):
        for t in range(nb):
            row = active[info[2 + j] * nb + t] - info[1]

            @pl.when(jnp.logical_and(row >= 0, row < rows))
            def _():
                for k in range(parts):
                    for i in range(tiles):
                        lines = turned[k, pl.ds(i * TILE * rows + row, TILE, stride=rows), :]
                        found[k, j * nb + t, i * TILE : (i + 1) * TILE, :] = lines

    def give(k):
        return pltpu.make_async_copy(found.at[k], pairs[k], sem_out.at[k])

    for k in range(parts):
        give(k).start()
    for k in range(parts):
        give(k).wait()
    if kept is not None:
        for i in range(tiles):
            keep(i).wait()


def extract(three_index, screen_mask, active, info, chunk, width, nb, keep):
    act, slab, rows = three_index.shape
    tiles = act // TILE
    parts = chunk // width
    out_shape = [jax.ShapeDtypeStruct((act, act, width), jnp.float32)] * parts
    if keep:
        out_shape.append(jax.ShapeDtypeStruct((act, chunk, rows), jnp.float32))
    smem, vmem, hbm, anywhere = places()
    return pl.pallas_call(
        functools.partial(extract_body, nb, parts),
        out_shape=out_shape,
        in_specs=[smem, smem, hbm, vmem],
        out_specs=[anywhere] * len(out_shape),
        scratch_shapes=[
            pltpu.VMEM((act, chunk, rows), jnp.float32),
            pltpu.VMEM((chunk // width, act * rows, width), jnp.float32),
            pltpu.VMEM((chunk // width, act, act, width), jnp.float32),
            pltpu.VMEM((chunk, rows), jnp.float32),
            pltpu.SemaphoreType.DMA((tiles,)),
            pltpu.SemaphoreType.DMA((parts,)),
            pltpu.SemaphoreType.DMA((tiles,)),
        ],
        compiler_params=pltpu.CompilerParams(vmem_limit_bytes=50 * MIB),
        cost_estimate=pl.CostEstimate(
            flops=4 * act * act * chunk * rows,
            transcendentals=0,
            bytes_accessed=4 * act * chunk * (act + rows * (2 if keep else 1)),
        ),
        name="extract",
    )(info, active, three_index, screen_mask)


def q_body(nb, count, info, three, screen, sib, *refs):
    blocks, (out, own, lhs, acc, mask, sems) = refs[: 2 * count], refs[2 * count :]
    act, depth, rows = own.shape
    chunk = depth // 2
    height = acc.shape[0]

    start = pl.multiple_of(info[0] * depth, depth)

    def bring(tile, i):
        return pltpu.make_async_copy(three.at[tile, pl.ds(start, depth), :], own.at[tile], sems.at[i])

    for i in range(act // TILE):
        bring(pl.ds(i * TILE, TILE), i).start()
    mask[...] = expand_mask(screen, info[0], depth, rows)
    lhs[...] = jnp.zeros_like(lhs)
    acc[...] = jnp.zeros_like(acc)
    nn = ((1,), (0,))

    @pl.loop(0, act // TILE)
    def _(i):
        tile = pl.ds(pl.multiple_of(i * TILE, TILE), TILE)
        for k in range(2):
            for j in range(count):
                for t in range(nb):
                    lhs[k, pl.ds(j * TILE + t, TILE, stride=height), :] = blocks[k * count + j][t, tile, :]
        pieces = [lhs[k, n * height : (n + 1) * height, :] for n in range(TILE) for k in range(2)]
        left, left_low = split(jnp.concatenate(pieces, axis=1))
        bring(tile, i).wait()
        right = [x.reshape(TILE * depth, rows) for x in (own[tile] * mask[...][None], sib[tile])]
        top, low = split(jnp.concatenate(right, axis=1))
        both = mxu(jnp.concatenate([left, left_low], axis=0), top, nn)
        acc[...] += both[:height] + both[height:] + mxu(left, low, nn)

    for j in range(count):
        where = pl.multiple_of(info[2 + j] * TILE, TILE)
        out[pl.ds(where, TILE), :] = acc[j * TILE : (j + 1) * TILE, :]


def q_partial(three_index, screen_mask, sib, blocks, info):
    act, depth, rows = sib.shape
    count = len(blocks[0])
    nb = act // count
    smem, vmem, hbm, anywhere = places()
    return pl.pallas_call(
        functools.partial(q_body, nb, count),
        out_shape=jax.ShapeDtypeStruct((count * TILE, 2 * rows), jnp.float32),
        in_specs=[smem, hbm, vmem, vmem] + [vmem] * (2 * count),
        out_specs=vmem,
        scratch_shapes=[
            pltpu.VMEM((act, depth, rows), jnp.float32),
            pltpu.VMEM((2, TILE * count * TILE, depth // 2), jnp.float32),
            pltpu.VMEM((count * TILE, 2 * rows), jnp.float32),
            pltpu.VMEM((depth, rows), jnp.float32),
            pltpu.SemaphoreType.DMA((act // TILE,)),
        ],
        compiler_params=pltpu.CompilerParams(vmem_limit_bytes=49 * MIB),
        cost_estimate=pl.CostEstimate(
            flops=12 * act * act * depth * rows,
            transcendentals=0,
            bytes_accessed=4 * act * depth * (act + 2 * rows),
        ),
        name="qpartial",
    )(info, three_index, screen_mask, sib, *[b.reshape(nb, act, depth // 2) for half in blocks for b in half])


def half_body(chips, info, own, twin, *refs):
    count = 2 * (chips - 1)
    blocks, outs = refs[:count], refs[count : count + 2]
    held, acc = refs[count + 2 :]
    size, chunk = blocks[0].shape
    rows, depth = own.shape

    def place(hops):
        return pl.ds(pl.multiple_of(info[2 + hops] * size, TILE), size)

    for n in range(count):
        j, k = n // 2, n % 2
        held[place(j if j < chips // 2 else j + 1), k * chunk : (k + 1) * chunk] = blocks[n][...]
    held[place(chips // 2), :] = jnp.zeros((size, 2 * chunk), jnp.float32)
    acc[...] = jnp.zeros_like(acc)
    nn = ((1,), (0,))
    step = 6 * LANES

    def add(start, length):
        top, low = split(held[pl.ds(start, length), :])
        for h, density in enumerate((own, twin)):
            left, left_low = split(density[:, pl.ds(start, length)])
            acc[h] += mxu(left, top, nn) + mxu(left_low, top, nn) + mxu(left, low, nn)

    @pl.loop(0, depth // step, unroll=True)
    def _(i):
        add(pl.multiple_of(i * step, step), step)

    if depth % step:
        add(depth - depth % step, depth % step)
    core = info[2 + chips]
    for first in range(2):

        @pl.when(core == first)
        def _():
            for k in range(2):
                for h in range(2):
                    at = (h ^ first) * rows
                    outs[k][at : at + rows, :] = acc[h, :, k * chunk : (k + 1) * chunk]


def half_partial(own, twin, blocks, info, chips):
    size, chunk = blocks[0].shape
    rows, depth = own.shape
    smem, vmem, hbm, anywhere = places()
    return pl.pallas_call(
        functools.partial(half_body, chips),
        out_shape=[jax.ShapeDtypeStruct((2 * rows, chunk), jnp.float32)] * 2,
        in_specs=[smem, vmem, vmem] + [vmem] * len(blocks),
        out_specs=[vmem, vmem],
        scratch_shapes=[
            pltpu.VMEM((depth, 2 * chunk), jnp.float32),
            pltpu.VMEM((2, rows, 2 * chunk), jnp.float32),
        ],
        compiler_params=pltpu.CompilerParams(vmem_limit_bytes=14 * MIB),
        cost_estimate=pl.CostEstimate(
            flops=24 * rows * depth * chunk,
            transcendentals=0,
            bytes_accessed=8 * rows * depth + 8 * depth * chunk,
        ),
        name="half",
    )(info, own, twin, *blocks)


def fast(orb, aux, three_index, pair_density, active_orbitals, screen_mask, one_density, inactive_fock, active_fock):
    act, slab, rows = three_index.shape
    inactive = active_fock.shape[1]
    chips = orb // 2
    nb = act // chips
    blk = nb * act
    depth = slab // 2
    chunk = depth // 2
    me = lax.axis_index("orb")
    chip, core = lax.shift_right_logical(me, 1), lax.bitwise_and(me, 1)
    half_chip = lax.shift_right_logical(chip, 1)
    sign = 1 - 2 * core
    first_row = me * rows

    order = list(range(0, chips, 2)) + list(range(chips - 1, 0, -2))
    position = jnp.where(lax.bitwise_and(chip, 1) == 0, half_chip, chips - 1 - half_chip)

    def chip_at(sgn, hops):
        place = lax.rem(position + sgn * hops + chips, chips)
        return jnp.where(place < chips // 2, 2 * place, 2 * chips - 1 - 2 * place)

    def info_of(sgn, half):
        by_hops = chip_at(sgn, jnp.arange(chips, dtype=jnp.int32))
        return jnp.concatenate([jnp.stack([half, first_row]), by_hops, core.reshape(1)]).astype(jnp.int32)

    near = [(order[k], order[(k + 1) % chips]) for k in range(chips)]
    ahead = [(2 * a, 2 * b) for a, b in near] + [(2 * b + 1, 2 * a + 1) for a, b in near]
    behind = [(b, a) for a, b in ahead]
    twin = [(i, i ^ 1) for i in range(orb)]

    def hop(x, pairs):
        return lax.ppermute(x, "orb", pairs)

    local_rows = jnp.arange(rows, dtype=jnp.int32)
    mine, theirs = info_of(sign, core), info_of(-sign, 1 - core)

    shells = screen_mask.T
    far = chips // 2
    def pick(info, keep):
        *found, last = extract(three_index, shells, active_orbitals, info, depth, chunk, nb, keep)
        flat = [f.reshape(act * act, chunk) for f in (found if keep else found + [last])]
        return flat, last

    other = hop(pair_density, twin)
    given, sib_three = pick(theirs, True)
    got = [hop(g, twin) for g in given]
    given, mine = lax.optimization_barrier((given, mine))
    found, _ = pick(mine, False)
    contributions = []
    for f, g in zip(found, got):
        contributions.append([f[j * blk : (j + 1) * blk] + g[j * blk : (j + 1) * blk] for j in range(chips)])
    inactive_fock, active_fock, contributions, other, sib_three = lax.optimization_barrier(
        (inactive_fock, active_fock, contributions, other, sib_three)
    )
    sib_three = hop(sib_three, twin)
    first = [(hop(c[far], ahead), hop(c[far + 1], behind)) for c in contributions]
    first, sib_three = lax.optimization_barrier((first, sib_three))
    totals = []
    for c, (a, b) in zip(contributions, first):
        for s in range(1, far):
            a = hop(a + c[far - s], ahead)
            if s < chips - 1 - far:
                b = hop(b + c[far + 1 + s], behind)
        totals.append(c[0] + a + b)

    far_at = chip_at(sign, far) * blk
    far_columns = [lax.dynamic_slice_in_dim(d, far_at, blk, 1) for d in (pair_density, other)]
    density_far = jnp.concatenate(
        [jnp.where(core == 0, far_columns[0], far_columns[1]), jnp.where(core == 0, far_columns[1], far_columns[0])],
        axis=0,
    )

    def gather(x):
        blocks = [None] * chips
        blocks[0] = a = b = x
        for s in range(1, far + 1):
            a = hop(a, ahead)
            blocks[(chips - s) % chips] = a
            if s < chips - far:
                b = hop(b, behind)
                blocks[s] = b
        return blocks

    gathered = [gather(x) for x in totals]
    near_blocks = [gathered[k][j] for j in range(chips) if j != far for k in range(2)]
    halves = half_partial(pair_density, other, near_blocks, mine, chips)
    halves = [h + jnp.dot(density_far, gathered[k][far], precision=HIGH) for k, h in enumerate(halves)]
    q = q_partial(three_index, shells, sib_three, [gather(x) for x in halves], mine)
    q = q.reshape(chips, TILE, 2 * rows)[:, :nb].reshape(act, 2 * rows)

    share = rows // aux
    aux_at = lax.axis_index("aux")

    def across(x, orb_bits, aux_bits):
        table = [(o * aux + y, (o ^ orb_bits) * aux + (y ^ aux_bits)) for o in range(orb) for y in range(aux)]
        return lax.ppermute(x, ("orb", "aux"), table)

    closed = 2.0 * (inactive_fock[:, :inactive] + active_fock)
    opened = jnp.dot(inactive_fock[:, inactive:], one_density, precision=HIGHEST)
    closed_twin = hop(closed, twin)
    closed_chip = jnp.concatenate(
        [jnp.where(core == 0, closed, closed_twin), jnp.where(core == 0, closed_twin, closed)], axis=0
    )

    once = (aux_at == 0).astype(jnp.float32)
    own_q, twin_q = q[:, :rows] + once * opened.T, q[:, rows:]
    occ_index = jnp.concatenate([jnp.arange(inactive, dtype=jnp.int32), active_orbitals])
    my_rows, twin_rows = first_row + local_rows, (me ^ 1) * rows + local_rows
    width = (inactive + act) // 2
    act_pick = (active_orbitals[:, None] == my_rows[None, :]).astype(jnp.float32) * once
    act_closed = jnp.pad(jnp.dot(act_pick, closed, precision=HIGHEST), ((0, 0), (0, act)))

    def picked(half):
        wanted = lax.dynamic_slice_in_dim(occ_index, half * width, width, 0)
        chosen = [(r[:, None] == wanted[None, :]).astype(jnp.float32) for r in (my_rows, twin_rows)]
        top = jnp.dot(jnp.concatenate([own_q, twin_q], axis=1), jnp.concatenate(chosen, axis=0), precision=HIGHEST)
        return jnp.concatenate([top, lax.dynamic_slice_in_dim(act_closed, half * width, width, 1)], axis=0)

    keep_occ, send_occ = picked(core), picked(1 - core)
    twin_q, keep_occ, send_occ = lax.optimization_barrier((twin_q, keep_occ, send_occ))
    occ = keep_occ + hop(send_occ, twin)

    q_mine = own_q + hop(twin_q, twin)
    sent = lax.dynamic_slice_in_dim(q_mine, (1 - aux_at) * share, share, 1)
    q_rows = lax.dynamic_slice_in_dim(q_mine, aux_at * share, share, 1) + across(sent, 0, 1)

    occ = occ + across(occ, 2, 0) + across(occ, 0, 1) + across(occ, 2, 1)
    occ = occ + across(occ, 4, 0) + across(occ, 8, 0) + across(occ, 12, 0)
    occ_twin = hop(occ, twin)
    occ = jnp.concatenate([jnp.where(core == 0, occ, occ_twin), jnp.where(core == 0, occ_twin, occ)], axis=1)

    upper = jnp.concatenate([closed_chip[:inactive].T, occ[act:, :inactive].T], axis=1)
    occupied = jnp.concatenate([upper, occ[:act]], axis=0)

    mine_at = aux_at * share
    fock_mine = jnp.concatenate([lax.dynamic_slice_in_dim(closed, mine_at, share, 0), q_rows.T], axis=1)
    pick_rows = (first_row + mine_at + jnp.arange(share, dtype=jnp.int32))[:, None] == occ_index[None, :]
    transposed = jnp.dot(pick_rows.astype(jnp.float32), occupied, precision=HIGHEST)
    return 2.0 * (fock_mine - transposed)


def plain(orb, aux, three_index, pair_density, active_orbitals, screen_mask, one_density, inactive_fock, active_fock):
    act_count = three_index.shape[0]
    slab_count = three_index.shape[1]
    row_count = three_index.shape[2]
    inactive_count = active_fock.shape[1]
    orb_position = lax.axis_index("orb")
    kept_mask = jnp.repeat(
        jnp.repeat(screen_mask.astype(jnp.float32), slab_count // screen_mask.shape[0], axis=0),
        row_count // screen_mask.shape[1],
        axis=1,
    )
    screened = three_index * kept_mask[None]
    global_rows = orb_position * row_count + jnp.arange(row_count, dtype=jnp.int32)
    active_pick = (global_rows[:, None] == active_orbitals[None, :]).astype(jnp.float32)
    partial_pairs = jnp.einsum("wPp,pv->Pvw", screened, active_pick, precision=HIGHEST).reshape(
        slab_count, act_count * act_count
    )
    pairs = lax.psum(partial_pairs, "orb")
    column_block = jnp.dot(pairs, pair_density.T, precision=HIGHEST)
    half = lax.all_gather(column_block, "orb", axis=1, tiled=True)
    q_partial = jnp.einsum(
        "uPp,Ptu->pt", screened, half.reshape(slab_count, act_count, act_count), precision=HIGHEST
    )
    occ_index = jnp.concatenate([jnp.arange(inactive_count, dtype=jnp.int32), active_orbitals])
    row_share = row_count // aux
    aux_offset = lax.axis_index("aux") * row_share
    qmatrix = lax.psum(q_partial, "aux")
    inactive_cols = 2.0 * (inactive_fock[:, :inactive_count] + active_fock)
    active_cols = jnp.dot(inactive_fock[:, inactive_count:], one_density, precision=HIGHEST) + qmatrix
    fock = jnp.concatenate([inactive_cols, active_cols], axis=1)
    occ_pick = (global_rows[:, None] == occ_index[None, :]).astype(jnp.float32)
    occupied = lax.psum(jnp.dot(occ_pick.T, fock, precision=HIGHEST), "orb")
    fock_mine = lax.dynamic_slice_in_dim(fock, aux_offset, row_share, 0)
    pick_mine = lax.dynamic_slice_in_dim(occ_pick, aux_offset, row_share, 0)
    transposed = jnp.dot(pick_mine, occupied.T, precision=HIGHEST)
    return 2.0 * (fock_mine - transposed)


def shards(orb, aux, *args):
    act, slab, rows = args[0].shape
    chips = orb // 2
    fits = orb == 16 and aux == 2 and act % chips == 0 and act % TILE == 0
    fits = fits and args[6].shape[1] <= 2 * rows and (args[6].shape[1] + act) % 2 == 0
    fits = fits and slab % (4 * LANES) == 0 and rows % LANES == 0
    return (fast if fits else plain)(orb, aux, *args)


def solution(mesh):
    in_specs = (
        P(None, "aux", "orb"),
        P("orb", None),
        P(),
        P("aux", "orb"),
        P(),
        P("orb", None),
        P("orb", None),
    )
    out_specs = P(("orb", "aux"), None)
    body = functools.partial(shards, mesh.shape["orb"], mesh.shape["aux"])
    return jax.shard_map(body, mesh=mesh, in_specs=in_specs, out_specs=out_specs, check_vma=False)
```
